256 devices in a mesh: wide: 32 (over y, x, core), narrow: 8 (over z).
Axes of the slice: x: 4, y: 4, z: 8, core: 2. Of those that a mesh axis runs over, the one named last changes fastest.
Arguments:
- expression: bfloat16 [4000, 393216], P(None, ('wide', 'narrow')), may hold values from -60 to 60
- sketch_map: bfloat16 [64, 4000], replicated, may hold values from -0.09375 to 0.09375
Outputs:
- projected: float32 [64, 4000], P(None, 'narrow')
The draws below stay inside these ranges and needn't reach their ends.
All inputs are finite; a program needn't handle non-finite values.
Results may differ from the reference program's by a relative error of at most 0.00037.
Values sent between devices are 32-bit elements; how exact they have to be, the bound alone decides.
No kernel may reach another device: no remote copies, remote signals or barrier semaphores. Data moves between devices by JAX's collectives and lax.ppermute only.
A program may use at most 64 MiB of HBM per device.

```python
import jax
import jax.numpy as jnp
from jax import lax

GENES = 4000
SKETCH = 64
CELLS = 393216


def draw_expression(key, part):
    first, second, third = jax.random.split(jax.random.fold_in(key, 17), 3)
    position = jnp.arange(CELLS, dtype=jnp.float32) / CELLS
    cell_scale = jnp.exp(jnp.log(10.0) * (0.5 * position + 0.5 * jax.random.uniform(second, (CELLS,), jnp.float32)))
    base = jnp.clip(jax.random.normal(first, (GENES, CELLS), jnp.float32), -6.0, 6.0)
    gene_scale = 0.5 + jax.random.uniform(third, (GENES,), jnp.float32)
    values = base * gene_scale[:, None] * cell_scale[None, :]
    return jnp.clip(values, -60.0, 60.0).astype(jnp.bfloat16)


def gaussian(own_key, extent, scale, most, kind=jnp.bfloat16):
    return jnp.clip(scale * jax.random.normal(own_key, extent, jnp.float32), -most, most).astype(kind)


def setup_inputs(seed: int = 0) -> dict:
    key_of = jax.random.split(jax.random.key(seed), 3)
    expression = draw_expression(jax.random.fold_in(key_of[2], 71), 0)
    sketch_map = gaussian(key_of[1], (SKETCH, GENES), GENES ** -0.5, 0.09375)
    return dict(expression=expression, sketch_map=sketch_map)


def reference(expression, sketch_map):
    sketched = jnp.dot(sketch_map.astype(jnp.float32), expression.astype(jnp.float32), preferred_element_type=jnp.float32).astype(jnp.bfloat16)
    gram = lax.dot_general(sketched.astype(jnp.float32), sketched.astype(jnp.float32), (((1,), (1,)), ((), ())), preferred_element_type=jnp.float32)
    lower = jnp.linalg.cholesky(gram)
    products = lax.dot_general(sketched.astype(jnp.float32), expression.astype(jnp.float32), (((1,), (1,)), ((), ())), preferred_element_type=jnp.float32)
    projected = lax.linalg.triangular_solve(lower, products, left_side=True, lower=True)
    return projected
```

```python
import functools

import jax
import jax.numpy as jnp
from jax import lax
from jax.experimental import pallas as pl
from jax.experimental.pallas import tpu as pltpu
from jax.sharding import Mesh
from jax.sharding import PartitionSpec as P

WIDE = ("y", "x", "c")
CELL_BLOCK = 512
SPAN = 256


def nn(a, b):
    return lax.dot_general(a, b, (((1,), (0,)), ((), ())), preferred_element_type=jnp.float32)


def nt(a, b):
    return lax.dot_general(a, b, (((1,), (1,)), ((), ())), preferred_element_type=jnp.float32)


def front_kernel(parts, share, s_ref, e_ref, mine_ref, theirs_ref, acc, gram):
    step = pl.program_id(0)
    rows, genes = s_ref.shape

    @pl.when(step == 0)
    def _():
        acc[...] = jnp.zeros_like(acc)
        gram[...] = jnp.zeros_like(gram)

    block = e_ref[...]
    sketched = nn(s_ref[...], block).astype(jnp.bfloat16)
    gram[...] += nt(sketched, sketched)
    acc[:, :genes] += nt(sketched, block)

    @pl.when(step == pl.num_programs(0) - 1)
    def _():
        me = lax.axis_index("c")
        for ref, core in ((mine_ref, me), (theirs_ref, 1 - me)):
            packed = [
                gram[pl.ds(pl.multiple_of(16 * j + 8 * core, 8), 8), :] for j in range(rows // 16)
            ]
            packed = jnp.concatenate(packed, axis=1)
            for z in range(parts):
                start = z * share
                base, shift = start // 128 * 128, start % 128
                wide = acc[:, pl.ds(pl.multiple_of(base + SPAN * core, 128), SPAN + 128)]
                ref[z, :rows, :] = wide[:, shift : shift + SPAN]
                ref[z, rows:, :] = packed


def front(sketch_map, expression, parts):
    rows, genes = sketch_map.shape
    cells = expression.shape[1]
    out = jax.ShapeDtypeStruct((parts, rows + 8, SPAN), jnp.float32)
    whole = pl.BlockSpec(out.shape, lambda i: (0, 0, 0))
    return pl.pallas_call(
        functools.partial(front_kernel, parts, genes // parts),
        grid=(cells // CELL_BLOCK,),
        in_specs=[
            pl.BlockSpec((rows, genes), lambda i: (0, 0)),
            pl.BlockSpec((genes, CELL_BLOCK), lambda i: (0, i)),
        ],
        out_specs=[whole, whole],
        out_shape=[out, out],
        scratch_shapes=[
            pltpu.VMEM((rows, pl.cdiv(genes, 128) * 128), jnp.float32),
            pltpu.VMEM((rows, rows), jnp.float32),
        ],
        compiler_params=pltpu.CompilerParams(vmem_limit_bytes=48 << 20),
        name="front",
    )(sketch_map, expression)


def tail_kernel(share, mine_ref, other_ref, out_ref):
    me = lax.axis_index("c")
    rows = out_ref.shape[0]
    mine, other = mine_ref[...], other_ref[...]
    pair = [jnp.where(me == 0, mine, other), jnp.where(me == 0, other, mine)]
    sub = lax.broadcasted_iota(jnp.int32, (8, 128), 0)
    lane = lax.broadcasted_iota(jnp.int32, (8, 128), 1)
    work = []
    for g in range(rows // 8):
        held = pair[g % 2][rows:, 128 * (g // 4) : 128 * (g // 4) + 128]
        if (g // 2) % 2 == 0:
            held = pltpu.roll(held, 64, 1)
        work.append(jnp.where(lane < 64, jnp.where(lane == sub + 8 * g, 1.0, 0.0), held))
    pivots = [jnp.ones((8, 128), jnp.float32) for _ in work]
    for k in range(rows):
        group, s = k // 8, k % 8
        row = jnp.broadcast_to(work[group][s : s + 1, :], (8, 128))
        pivot = jnp.broadcast_to(row[:, 64 + k : 65 + k], (8, 128))
        pivots[group] = jnp.where(sub == s, pivot, pivots[group])
        scaled = row * (1.0 / pivot)
        for g in range(group, rows // 8):
            column = jnp.broadcast_to(work[g][:, 64 + k : 65 + k], (8, 128))
            if g == group:
                column = jnp.where(sub > s, column, 0.0)
            work[g] = work[g] - column * scaled
    inverse = [w * lax.rsqrt(p) for w, p in zip(work, pivots)]
    inverse = jnp.concatenate(inverse, axis=0)[:, :64]
    genes = jnp.concatenate([pair[0][:rows], pair[1][:rows]], axis=1)
    solved = lax.dot_general(
        inverse,
        genes,
        (((1,), (0,)), ((), ())),
        precision=lax.Precision.HIGHEST,
        preferred_element_type=jnp.float32,
    )
    out_ref[...] = solved[:, :share]


def tail(mine, other, rows, share):
    return pl.pallas_call(
        functools.partial(tail_kernel, share),
        in_specs=[pl.BlockSpec(memory_space=pltpu.VMEM)] * 2,
        out_specs=pl.BlockSpec(memory_space=pltpu.VMEM),
        out_shape=jax.ShapeDtypeStruct((rows, share), jnp.float32),
        name="tail",
    )(mine, other)


def wide_pairs(first, second):
    pairs = []
    for y in range(4):
        for x in range(4):
            for c, (ty, tx) in enumerate((first(y, x), second(y, x))):
                pairs.append(((y * 4 + x) * 2 + c, (ty * 4 + tx) * 2 + c))
    return pairs


def near(v):
    return v ^ 1


def across(v):
    return 3 - v


def on_device(expression, sketch_map):
    rows, genes = sketch_map.shape
    parts = lax.axis_size("z")
    mine, theirs = front(sketch_map, expression, parts)
    swap = [(0, 1), (1, 0)]
    summed = mine + lax.ppermute(theirs, "c", swap)
    total = lax.all_to_all(summed, "z", 0, 0, tiled=True).sum(axis=0)
    steps = (
        (lambda y, x: (y, near(x)), lambda y, x: (near(y), x)),
        (lambda y, x: (y, across(x)), lambda y, x: (across(y), x)),
        (lambda y, x: (near(y), x), lambda y, x: (y, near(x))),
        (lambda y, x: (across(y), x), lambda y, x: (y, across(x))),
    )
    for first, second in steps:
        total = total + lax.ppermute(total, WIDE, wide_pairs(first, second))
    other = lax.ppermute(total, "c", swap)
    return tail(total, other, rows, genes // parts)


def solution(mesh):
    grid = Mesh(mesh.devices.reshape(4, 4, 2, 8), ("y", "x", "c", "z"))
    placed = (P(None, ("y", "x", "c", "z")), P())
    return jax.shard_map(
        on_device, mesh=grid, in_specs=placed, out_specs=P(None, "z"), check_vma=False
    )
```

```python
import functools

import jax
import jax.numpy as jnp
from jax import lax
from jax.experimental import pallas as pl
from jax.experimental.pallas import tpu as pltpu
from jax.sharding import Mesh
from jax.sharding import PartitionSpec as P

WIDE = ("y", "x", "c")
CHUNKS = (512, 512, 512)
SPAN = 256


def nn(a, b):
    return lax.dot_general(a, b, (((1,), (0,)), ((), ())), preferred_element_type=jnp.float32)


def nt(a, b):
    return lax.dot_general(a, b, (((1,), (1,)), ((), ())), preferred_element_type=jnp.float32)


def front_kernel(parts, share, s_hbm, e_hbm, mine_ref, theirs_ref, s_ref, *scratch):
    count = len(CHUNKS)
    blocks = scratch[:count]
    acc, gram, sems = scratch[count:]
    rows, genes = s_ref.shape
    copies = [pltpu.make_async_copy(s_hbm, s_ref, sems.at[count])]
    start = 0
    for i, size in enumerate(CHUNKS):
        copies.append(
            pltpu.make_async_copy(e_hbm.at[:, pl.ds(start, size)], blocks[i], sems.at[i])
        )
        start += size
    for copy in copies:
        copy.start()
    acc[:, genes:] = jnp.zeros((rows, acc.shape[1] - genes), jnp.float32)
    copies[0].wait()
    total = None
    for i in range(count):
        copies[i + 1].wait()
        block = blocks[i][...]
        sketched = nn(s_ref[...], block).astype(jnp.bfloat16)
        square = nt(sketched, sketched)
        total = square if i == 0 else total + square
        if i == 0:
            acc[:, :genes] = nt(sketched, block)
        else:
            acc[:, :genes] += nt(sketched, block)
    half = rows // 2
    gram[...] = jnp.concatenate([total[:half], total[half:]], axis=1)
    me = lax.axis_index("c")
    for ref, core in ((mine_ref, me), (theirs_ref, 1 - me)):
        for z in range(parts):
            base, shift = z * share // 128 * 128, z * share % 128
            wide = acc[:, pl.ds(pl.multiple_of(base + SPAN * core, 128), SPAN + 128)]
            part = wide[:, shift : shift + SPAN]
            for m in range(rows // 4):
                r, c = m // 2 * 8, m % 2 * 128
                ref[m, 8 * z : 8 * z + 8, :] = part[r : r + 8, c : c + 128]
        for m in range(rows // 4):
            row = gram[pl.ds(2 * m + core, 1), :]
            ref[m, 8 * parts :, :] = jnp.broadcast_to(row, (8, 128))


def front(sketch_map, expression, parts):
    rows, genes = sketch_map.shape
    out = jax.ShapeDtypeStruct((rows // 4, 8 * parts + 8, 128), jnp.float32)
    return pl.pallas_call(
        functools.partial(front_kernel, parts, genes // parts),
        in_specs=[pl.BlockSpec(memory_space=pltpu.HBM)] * 2,
        out_specs=[pl.BlockSpec(memory_space=pltpu.VMEM)] * 2,
        out_shape=[out, out],
        scratch_shapes=[pltpu.VMEM((rows, genes), jnp.bfloat16)]
        + [pltpu.VMEM((genes, size), jnp.bfloat16) for size in CHUNKS]
        + [
            pltpu.VMEM((rows, pl.cdiv(genes, 128) * 128), jnp.float32),
            pltpu.VMEM((rows // 2, 2 * rows), jnp.float32),
            pltpu.SemaphoreType.DMA((len(CHUNKS) + 1,)),
        ],
        compiler_params=pltpu.CompilerParams(vmem_limit_bytes=40 << 20),
        name="front",
    )(
        pltpu.with_memory_space_constraint(sketch_map, pltpu.HBM),
        pltpu.with_memory_space_constraint(expression, pltpu.HBM),
    )


def added(ref, where):
    parts = [ref[i, where, :] for i in range(ref.shape[0])]
    while len(parts) > 1:
        parts = [a + b for a, b in zip(parts[::2], parts[1::2])]
    return parts[0]


def spread_kernel(in_ref, out_ref):
    parts = out_ref.shape[0]
    square = added(in_ref, slice(8 * parts, 8 * parts + 8))
    for z in range(parts):
        out_ref[z, :8, :] = added(in_ref, slice(8 * z, 8 * z + 8))
        out_ref[z, 8:, :] = square


def repeat_kernel(in_ref, out_ref):
    whole = added(in_ref, slice(None))
    for i in range(out_ref.shape[0]):
        out_ref[i] = whole


def small(kernel, shape, name, *args):
    return pl.pallas_call(
        kernel,
        in_specs=[pl.BlockSpec(memory_space=pltpu.VMEM)] * len(args),
        out_specs=pl.BlockSpec(memory_space=pltpu.VMEM),
        out_shape=jax.ShapeDtypeStruct(shape, jnp.float32),
        name=name,
    )(*args)


def over_tile(x):
    return jnp.broadcast_to(x, (8, 128))


def inverse_factor(work, sub):
    count = len(work)
    for g in range(count):
        block = work[g]
        at = 64 + 8 * g
        columns = [over_tile(block[:, at + j : at + j + 1]) for j in range(8)]
        a = {(i, j): over_tile(columns[j][i : i + 1]) for j in range(8) for i in range(j, 8)}
        rows = [over_tile(block[i : i + 1]) for i in range(8)]
        low, inverse = {}, []
        for j in range(8):
            inverse.append(1.0 / a[j, j])
            for i in range(j + 1, 8):
                low[i, j] = a[i, j] * inverse[j]
            for i in range(j + 1, 8):
                for m in range(j + 1, i + 1):
                    a[i, m] = a[i, m] - low[i, j] * a[m, j]
        solved = []
        for i in range(8):
            row = rows[i]
            for j in range(i):
                row = row - low[i, j] * solved[j]
            solved.append(row)
        if g < count - 1:
            back = [None] * 8
            for i in reversed(range(8)):
                row = solved[i] * inverse[i]
                for j in range(i + 1, 8):
                    row = row - low[j, i] * back[j]
                back[i] = row
            for h in range(g + 1, count):
                left = work[h]
                for j in range(8):
                    left = left - over_tile(work[h][:, at + j : at + j + 1]) * back[j]
                work[h] = left
        block, pivots = solved[0], a[0, 0]
        for i in range(1, 8):
            block = jnp.where(sub == i, solved[i], block)
            pivots = jnp.where(sub == i, a[i, i], pivots)
        work[g] = block * lax.rsqrt(pivots)
    return work


def tail_kernel(in_ref, out_ref):
    rows, share = out_ref.shape
    sub = lax.broadcasted_iota(jnp.int32, (8, 128), 0)
    lane = lax.broadcasted_iota(jnp.int32, (8, 128), 1)
    gram = in_ref[:, 8, :]
    work = []
    for g in range(rows // 8):
        held = gram[8 * (g % 4) : 8 * (g % 4) + 8]
        if g < 4:
            held = pltpu.roll(held, 64, 1)
        work.append(jnp.where(lane < 64, jnp.where(lane == sub + 8 * g, 1.0, 0.0), held))
    inverse = jnp.concatenate(inverse_factor(work, sub), axis=0)[:, :rows]
    genes = jnp.concatenate(
        [
            jnp.concatenate([in_ref[(2 * r + h) * 2 + c, :8, :] for r in range(rows // 8)], axis=0)
            for c in range(2)
            for h in range(2)
        ],
        axis=1,
    )
    solved = lax.dot_general(
        inverse,
        genes,
        (((1,), (0,)), ((), ())),
        precision=lax.Precision.HIGHEST,
        preferred_element_type=jnp.float32,
    )
    out_ref[...] = solved[:, :share]


def on_device(expression, sketch_map):
    rows, genes = sketch_map.shape
    parts = lax.axis_size("z")
    mine, theirs = front(sketch_map, expression, parts)
    summed = mine + lax.ppermute(theirs, "c", [(0, 1), (1, 0)])
    arrived = lax.all_to_all(summed, ("y", "x"), 0, 0, tiled=True)
    piece = small(spread_kernel, (parts, 16, 128), "spread", arrived)
    arrived = lax.all_to_all(piece, "z", 0, 0, tiled=True)
    piece = small(repeat_kernel, (lax.axis_size(WIDE), 16, 128), "repeat", arrived)
    arrived = lax.all_to_all(piece, WIDE, 0, 0, tiled=True)
    return small(tail_kernel, (rows, genes // parts), "tail", arrived)


def solution(mesh):
    grid = Mesh(mesh.devices.reshape(4, 4, 2, 8), ("y", "x", "c", "z"))
    placed = (P(None, ("y", "x", "c", "z")), P())
    return jax.shard_map(
        on_device, mesh=grid, in_specs=placed, out_specs=P(None, "z"), check_vma=False
    )
```

```python
import functools

import jax
import jax.numpy as jnp
from jax import lax
from jax.experimental import pallas as pl
from jax.experimental.pallas import tpu as pltpu
from jax.sharding import Mesh
from jax.sharding import PartitionSpec as P

WIDE = ("y", "x", "c")
CHUNKS = (512, 512, 512)
SPAN = 256


def nn(a, b):
    return lax.dot_general(a, b, (((1,), (0,)), ((), ())), preferred_element_type=jnp.float32)


def nt(a, b):
    return lax.dot_general(a, b, (((1,), (1,)), ((), ())), preferred_element_type=jnp.float32)


def front_kernel(parts, share, s_hbm, e_hbm, mine_ref, theirs_ref, s_ref, *scratch):
    count = len(CHUNKS)
    blocks = scratch[:count]
    acc, gram, sems = scratch[count:]
    rows, genes = s_ref.shape
    copies = [pltpu.make_async_copy(s_hbm, s_ref, sems.at[count])]
    start = 0
    for i, size in enumerate(CHUNKS):
        copies.append(
            pltpu.make_async_copy(e_hbm.at[:, pl.ds(start, size)], blocks[i], sems.at[i])
        )
        start += size
    for copy in copies:
        copy.start()
    acc[:, genes:] = jnp.zeros((rows, acc.shape[1] - genes), jnp.float32)
    copies[0].wait()
    total = None
    for i in range(count):
        copies[i + 1].wait()
        block = blocks[i][...]
        sketched = nn(s_ref[...], block).astype(jnp.bfloat16)
        square = nt(sketched, sketched)
        total = square if i == 0 else total + square
        if i == 0:
            acc[:, :genes] = nt(sketched, block)
        else:
            acc[:, :genes] += nt(sketched, block)
    quarter = rows // 4
    for h in range(2):
        top = total[2 * quarter * h : 2 * quarter * h + quarter]
        low = total[2 * quarter * h + quarter : 2 * quarter * (h + 1)]
        gram[quarter * h : quarter * (h + 1), :] = jnp.concatenate([top, low], axis=1)
    me = lax.axis_index("c")
    for ref, core in ((mine_ref, me), (theirs_ref, 1 - me)):
        for z in range(parts):
            base, shift = z * share // 128 * 128, z * share % 128
            wide = acc[:, pl.ds(pl.multiple_of(base + SPAN * core, 128), SPAN + 128)]
            part = wide[:, shift : shift + SPAN]
            for m in range(rows // 4):
                r, c = m // 2 * 8, m % 2 * 128
                ref[m, 8 * z : 8 * z + 8, :] = part[r : r + 8, c : c + 128]
        half = gram[pl.ds(pl.multiple_of(quarter * core, 8), quarter), :]
        for m in range(quarter):
            ref[m, 8 * parts :, :] = half


def front(sketch_map, expression, parts):
    rows, genes = sketch_map.shape
    out = jax.ShapeDtypeStruct((rows // 4, 8 * parts + rows // 4, 128), jnp.float32)
    return pl.pallas_call(
        functools.partial(front_kernel, parts, genes // parts),
        in_specs=[pl.BlockSpec(memory_space=pltpu.HBM)] * 2,
        out_specs=[pl.BlockSpec(memory_space=pltpu.VMEM)] * 2,
        out_shape=[out, out],
        scratch_shapes=[pltpu.VMEM((rows, genes), jnp.bfloat16)]
        + [pltpu.VMEM((genes, size), jnp.bfloat16) for size in CHUNKS]
        + [
            pltpu.VMEM((rows, pl.cdiv(genes, 128) * 128), jnp.float32),
            pltpu.VMEM((rows // 2, 2 * rows), jnp.float32),
            pltpu.SemaphoreType.DMA((len(CHUNKS) + 1,)),
        ],
        compiler_params=pltpu.CompilerParams(vmem_limit_bytes=40 << 20),
        name="front",
    )(
        pltpu.with_memory_space_constraint(sketch_map, pltpu.HBM),
        pltpu.with_memory_space_constraint(expression, pltpu.HBM),
    )


def small(kernel, shape, name, *args):
    return pl.pallas_call(
        kernel,
        in_specs=[pl.BlockSpec(memory_space=pltpu.VMEM)] * len(args),
        out_specs=pl.BlockSpec(memory_space=pltpu.VMEM),
        out_shape=jax.ShapeDtypeStruct(shape, jnp.float32),
        name=name,
    )(*args)


def over_tile(x):
    return jnp.broadcast_to(x, (8, 128))


def inverse_factor(work, sub):
    count = len(work)
    for g in range(count):
        block = work[g]
        at = 64 + 8 * g
        columns = [over_tile(block[:, at + j : at + j + 1]) for j in range(8)]
        a = {(i, j): over_tile(columns[j][i : i + 1]) for j in range(8) for i in range(j, 8)}
        rows = [over_tile(block[i : i + 1]) for i in range(8)]
        low, inverse = {}, []
        for j in range(8):
            inverse.append(1.0 / a[j, j])
            for i in range(j + 1, 8):
                low[i, j] = a[i, j] * inverse[j]
            for i in range(j + 1, 8):
                for m in range(j + 1, i + 1):
                    a[i, m] = a[i, m] - low[i, j] * a[m, j]
        solved = []
        for i in range(8):
            row = rows[i]
            for j in range(i):
                row = row - low[i, j] * solved[j]
            solved.append(row)
        if g < count - 1:
            back = [None] * 8
            for i in reversed(range(8)):
                row = solved[i] * inverse[i]
                for j in range(i + 1, 8):
                    row = row - low[j, i] * back[j]
                back[i] = row
            for h in range(g + 1, count):
                left = work[h]
                for j in range(8):
                    left = left - over_tile(work[h][:, at + j : at + j + 1]) * back[j]
                work[h] = left
        block, pivots = solved[0], a[0, 0]
        for i in range(1, 8):
            block = jnp.where(sub == i, solved[i], block)
            pivots = jnp.where(sub == i, a[i, i], pivots)
        work[g] = block * lax.rsqrt(pivots)
    return work


def factor_kernel(mine_ref, other_ref, out_ref):
    me = lax.axis_index("c")
    mine, other = mine_ref[...], other_ref[...]
    halves = [jnp.where(me == 0, mine, other), jnp.where(me == 0, other, mine)]
    sub = lax.broadcasted_iota(jnp.int32, (8, 128), 0)
    lane = lax.broadcasted_iota(jnp.int32, (8, 128), 1)
    work = []
    for g in range(8):
        held = halves[g // 4][8 * (g % 2) : 8 * (g % 2) + 8]
        if g // 2 % 2 == 0:
            held = pltpu.roll(held, 64, 1)
        work.append(jnp.where(lane < 64, jnp.where(lane == sub + 8 * g, 1.0, 0.0), held))
    for g, block in enumerate(inverse_factor(work, sub)):
        out_ref[8 * g : 8 * g + 8, :] = block[:, :64]


def apply_kernel(inverse_ref, in_ref, out_ref):
    rows, share = out_ref.shape
    genes = jnp.concatenate(
        [
            jnp.concatenate([in_ref[(2 * r + h) * 2 + c] for r in range(rows // 8)], axis=0)
            for c in range(2)
            for h in range(2)
        ],
        axis=1,
    )
    solved = lax.dot_general(
        inverse_ref[...],
        genes,
        (((1,), (0,)), ((), ())),
        precision=lax.Precision.HIGHEST,
        preferred_element_type=jnp.float32,
    )
    out_ref[...] = solved[:, :share]


def on_device(expression, sketch_map):
    rows, genes = sketch_map.shape
    parts = lax.axis_size("z")
    swap = [(0, 1), (1, 0)]
    mine, theirs = front(sketch_map, expression, parts)
    summed = mine + lax.ppermute(theirs, "c", swap)
    total = lax.all_to_all(summed, ("y", "x"), 0, 0, tiled=True).sum(axis=0)
    ours = total[: 8 * parts].reshape(parts, 8, 128)
    square = jnp.broadcast_to(total[None, 8 * parts :], (parts, rows // 4, 128))
    piece = jnp.concatenate([ours, square], axis=1)
    piece = lax.all_to_all(piece, "z", 0, 0, tiled=True).sum(axis=0)
    spread = jnp.broadcast_to(piece[None, :8], (lax.axis_size(WIDE), 8, 128))
    gathered = lax.all_to_all(spread, WIDE, 0, 0, tiled=True)
    square = piece[8:]
    inverse = small(
        factor_kernel, (rows, rows), "factor", square, lax.ppermute(square, "c", swap)
    )
    return small(apply_kernel, (rows, genes // parts), "apply", inverse, gathered)


def solution(mesh):
    grid = Mesh(mesh.devices.reshape(4, 4, 2, 8), ("y", "x", "c", "z"))
    placed = (P(None, ("y", "x", "c", "z")), P())
    return jax.shard_map(
        on_device, mesh=grid, in_specs=placed, out_specs=P(None, "z"), check_vma=False
    )
```

```python
import functools

import jax
import jax.numpy as jnp
from jax import lax
from jax.experimental import pallas as pl
from jax.experimental.pallas import tpu as pltpu
from jax.sharding import Mesh
from jax.sharding import PartitionSpec as P

WIDE = ("y", "x", "c")
CHUNKS = (512, 512, 512)
EARLY = (0, 1024, 2048, 3072)


def nn(a, b):
    return lax.dot_general(a, b, (((1,), (0,)), ((), ())), preferred_element_type=jnp.float32)


def nt(a, b):
    return lax.dot_general(a, b, (((1,), (1,)), ((), ())), preferred_element_type=jnp.float32)


def front_kernel(parts, share, s_hbm, e_hbm, out_ref, s_ref, *scratch):
    count = len(CHUNKS)
    blocks = scratch[:count]
    acc, sems = scratch[count:]
    rows, genes = s_ref.shape
    first = [pltpu.make_async_copy(s_hbm, s_ref, sems.at[count])]
    for i, low in enumerate(EARLY):
        size = (EARLY + (genes,))[i + 1] - low
        first.append(
            pltpu.make_async_copy(
                e_hbm.at[pl.ds(low, size), pl.ds(0, CHUNKS[0])],
                blocks[0].at[pl.ds(low, size)],
                sems.at[count + 1 + i],
            )
        )
    start, later = CHUNKS[0], []
    for i, size in enumerate(CHUNKS[1:]):
        later.append(
            pltpu.make_async_copy(e_hbm.at[:, pl.ds(start, size)], blocks[i + 1], sems.at[i])
        )
        start += size
    for copy in first + later:
        copy.start()
    acc[:, genes:] = jnp.zeros((rows, acc.shape[1] - genes), jnp.float32)
    first[0].wait()
    square = None
    for i in range(count):
        if i == 0:
            sketched = None
            for j, low in enumerate(EARLY):
                first[j + 1].wait()
                high = (EARLY + (genes,))[j + 1]
                term = nn(s_ref[:, low:high], blocks[0][low:high, :])
                sketched = term if j == 0 else sketched + term
        else:
            later[i - 1].wait()
            sketched = nn(s_ref[...], blocks[i][...])
        sketched = sketched.astype(jnp.bfloat16)
        term = nt(sketched, sketched)
        square = term if i == 0 else square + term
        if i == 0:
            acc[:, :genes] = nt(sketched, blocks[i][...])
        else:
            acc[:, :genes] += nt(sketched, blocks[i][...])
    lane = lax.broadcasted_iota(jnp.int32, (8, 128), 1)
    for z in range(parts):
        base, shift = z * share // 128, z * share % 128
        for r in range(rows // 8):
            held = [
                acc[8 * r : 8 * r + 8, 128 * (base + t) : 128 * (base + t) + 128]
                for t in range(5 if shift else 4)
            ]
            if shift:
                held = [pltpu.roll(h, 128 - shift, 1) for h in held]
                held = [jnp.where(lane < 128 - shift, p, q) for p, q in zip(held, held[1:])]
            for t in range(4):
                out_ref[t // 2, 2 * r + t % 2, 8 * z : 8 * z + 8, :] = held[t]
    quarter = rows // 4
    for h in range(2):
        top = square[2 * quarter * h : 2 * quarter * h + quarter]
        low = square[2 * quarter * h + quarter : 2 * quarter * (h + 1)]
        half = jnp.concatenate([top, low], axis=1)
        for m in range(quarter):
            out_ref[h, m, 8 * parts :, :] = half


def front(sketch_map, expression, parts):
    rows, genes = sketch_map.shape
    return pl.pallas_call(
        functools.partial(front_kernel, parts, genes // parts),
        in_specs=[pl.BlockSpec(memory_space=pltpu.HBM)] * 2,
        out_specs=pl.BlockSpec(memory_space=pltpu.VMEM),
        out_shape=pltpu.VMEM((2, rows // 4, 8 * parts + rows // 4, 128), jnp.float32),
        scratch_shapes=[pltpu.VMEM((rows, genes), jnp.bfloat16)]
        + [pltpu.VMEM((genes, size), jnp.bfloat16) for size in CHUNKS]
        + [
            pltpu.VMEM((rows, parts // 2 * 1024 + 128), jnp.float32),
            pltpu.SemaphoreType.DMA((len(CHUNKS) + 1 + len(EARLY),)),
        ],
        compiler_params=pltpu.CompilerParams(vmem_limit_bytes=40 << 20),
        name="front",
    )(
        pltpu.with_memory_space_constraint(sketch_map, pltpu.HBM),
        pltpu.with_memory_space_constraint(expression, pltpu.HBM),
    )


def small(kernel, shape, name, *args, space=jax.ShapeDtypeStruct):
    return pl.pallas_call(
        kernel,
        in_specs=[pl.BlockSpec(memory_space=pltpu.VMEM)] * len(args),
        out_specs=pl.BlockSpec(memory_space=pltpu.VMEM),
        out_shape=space(shape, jnp.float32),
        name=name,
    )(*args)


def over_tile(x):
    return jnp.broadcast_to(x, (8, 128))


def inverse_factor(work, sub):
    count = len(work)
    for g in range(count):
        block = work[g]
        at = 64 + 8 * g
        columns = [over_tile(block[:, at + j : at + j + 1]) for j in range(8)]
        a = {(i, j): over_tile(columns[j][i : i + 1]) for j in range(8) for i in range(j, 8)}
        rows = [over_tile(block[i : i + 1]) for i in range(8)]
        low, inverse = {}, []
        for j in range(8):
            inverse.append(1.0 / a[j, j])
            for i in range(j + 1, 8):
                low[i, j] = a[i, j] * inverse[j]
            for i in range(j + 1, 8):
                for m in range(j + 1, i + 1):
                    a[i, m] = a[i, m] - low[i, j] * a[m, j]
        solved = []
        for i in range(8):
            row = rows[i]
            for j in range(i):
                row = row - low[i, j] * solved[j]
            solved.append(row)
        if g < count - 1:
            back = [None] * 8
            for i in reversed(range(8)):
                row = solved[i] * inverse[i]
                for j in range(i + 1, 8):
                    row = row - low[j, i] * back[j]
                back[i] = row
            for h in range(g + 1, count):
                left = work[h]
                for j in range(8):
                    left = left - over_tile(work[h][:, at + j : at + j + 1]) * back[j]
                work[h] = left
        block, pivots = solved[0], a[0, 0]
        for i in range(1, 8):
            block = jnp.where(sub == i, solved[i], block)
            pivots = jnp.where(sub == i, a[i, i], pivots)
        work[g] = block * lax.rsqrt(pivots)
    return work


def factor_kernel(mine_ref, other_ref, out_ref):
    me = lax.axis_index("c")
    mine, other = mine_ref[...], other_ref[...]
    halves = [jnp.where(me == 0, mine, other), jnp.where(me == 0, other, mine)]
    sub = lax.broadcasted_iota(jnp.int32, (8, 128), 0)
    lane = lax.broadcasted_iota(jnp.int32, (8, 128), 1)
    work = []
    for g in range(8):
        held = halves[g // 4][8 * (g % 2) : 8 * (g % 2) + 8]
        if g // 2 % 2 == 0:
            held = pltpu.roll(held, 64, 1)
        work.append(jnp.where(lane < 64, jnp.where(lane == sub + 8 * g, 1.0, 0.0), held))
    for g, block in enumerate(inverse_factor(work, sub)):
        out_ref[8 * g : 8 * g + 8, :] = block[:, :64]


def apply_kernel(inverse_ref, in_ref, out_ref):
    rows, share = out_ref.shape
    genes = jnp.concatenate(
        [
            jnp.concatenate([in_ref[(2 * r + h) * 2 + c] for r in range(rows // 8)], axis=0)
            for c in range(2)
            for h in range(2)
        ],
        axis=1,
    )
    solved = lax.dot_general(
        inverse_ref[...],
        genes,
        (((1,), (0,)), ((), ())),
        precision=lax.Precision.HIGHEST,
        preferred_element_type=jnp.float32,
    )
    out_ref[...] = solved[:, :share]


def near(x):
    return pltpu.with_memory_space_constraint(x, pltpu.VMEM)


def on_device(expression, sketch_map):
    rows, genes = sketch_map.shape
    parts = lax.axis_size("z")
    swap = [(0, 1), (1, 0)]
    me = lax.axis_index("c")
    halves = front(sketch_map, expression, parts)
    mine = lax.dynamic_index_in_dim(halves, me, 0, keepdims=False)
    theirs = lax.dynamic_index_in_dim(halves, 1 - me, 0, keepdims=False)
    summed = mine + lax.ppermute(theirs, "c", swap)
    total = lax.all_to_all(summed, ("y", "x"), 0, 0, tiled=True).sum(axis=0)
    ours = total[: 8 * parts].reshape(parts, 8, 128)
    square = jnp.broadcast_to(total[None, 8 * parts :], (parts, rows // 4, 128))
    piece = jnp.concatenate([ours, square], axis=1)
    piece = lax.all_to_all(piece, "z", 0, 0, tiled=True).sum(axis=0)
    spread = jnp.broadcast_to(piece[None, :8], (lax.axis_size(WIDE), 8, 128))
    gathered = near(lax.all_to_all(near(spread), WIDE, 0, 0, tiled=True))
    square = piece[8:]
    other = near(lax.ppermute(square, "c", swap))
    inverse = small(
        factor_kernel, (rows, rows), "factor", near(square), other, space=pltpu.VMEM
    )
    return small(apply_kernel, (rows, genes // parts), "apply", near(inverse), gathered)


def solution(mesh):
    grid = Mesh(mesh.devices.reshape(4, 4, 2, 8), ("y", "x", "c", "z"))
    placed = (P(None, ("y", "x", "c", "z")), P())
    return jax.shard_map(
        on_device, mesh=grid, in_specs=placed, out_specs=P(None, "z"), check_vma=False
    )
```

```python
import functools

import jax
import jax.numpy as jnp
from jax import lax
from jax.experimental import pallas as pl
from jax.experimental.pallas import tpu as pltpu
from jax.sharding import Mesh
from jax.sharding import PartitionSpec as P

WIDE = ("y", "x", "c")
PIECES = (1024, 1024, 1024, 928)
BLOCKS = (512, 512, 512)
SPAN = 256


def nn(a, b):
    return lax.dot_general(a, b, (((1,), (0,)), ((), ())), preferred_element_type=jnp.float32)


def nt(a, b):
    return lax.dot_general(a, b, (((1,), (1,)), ((), ())), preferred_element_type=jnp.float32)


def window_start(z, share):
    return z * share // 16 * 16


def put_products(ref, core, parts, share, sketched, e_ref, cells=slice(None), add=False):
    for z in range(parts):
        start = pl.multiple_of(window_start(z, share) + SPAN * core, 16)
        part = nt(sketched, e_ref[pl.ds(start, SPAN), cells])
        for m in range(ref.shape[0]):
            r, c = m // 2 * 8, m % 2 * 128
            tile = part[r : r + 8, c : c + 128]
            if add:
                tile = ref[m, 8 * z : 8 * z + 8, :] + tile
            ref[m, 8 * z : 8 * z + 8, :] = tile


def put_gram(ref, core, parts, gram_ref):
    half = gram_ref[core]
    for m in range(ref.shape[0]):
        ref[m, 8 * parts :, :] = half


def begin_kernel(parts, share, s_hbm, e_hbm, theirs_ref, sketched_ref, gram_ref, e_ref, *scratch):
    s_ref, acc, sems = scratch
    count = len(PIECES)
    spans = [slice(sum(PIECES[:i]), sum(PIECES[: i + 1])) for i in range(count)]
    blocks = [slice(sum(BLOCKS[:j]), sum(BLOCKS[: j + 1])) for j in range(len(BLOCKS))]
    whole = pltpu.make_async_copy(s_hbm, s_ref, sems.at[count * len(BLOCKS)])
    whole.start()
    copies = []
    for j, block in enumerate(blocks):
        for i, span in enumerate(spans):
            where = (pl.ds(span.start, PIECES[i]), pl.ds(block.start, BLOCKS[j]))
            copy = pltpu.make_async_copy(e_hbm.at[where], e_ref.at[where], sems.at[j * count + i])
            copy.start()
            copies.append(copy)
    whole.wait()
    core = 1 - lax.axis_index("c")
    square = None
    for j, block in enumerate(blocks):
        for i, span in enumerate(spans):
            copies[j * count + i].wait()
            term = nn(s_ref[:, span], e_ref[span, block])
            if i > 0:
                term = acc[:, : BLOCKS[j]] + term
            if i < count - 1:
                acc[:, : BLOCKS[j]] = term
        sketched = term.astype(jnp.bfloat16)
        sketched_ref[:, block] = sketched
        term = nt(sketched, sketched)
        square = term if j == 0 else square + term
        put_products(theirs_ref, core, parts, share, sketched, e_ref, block, j > 0)
    quarter = square.shape[0] // 4
    for h in range(2):
        top = square[2 * quarter * h : 2 * quarter * h + quarter]
        low = square[2 * quarter * h + quarter : 2 * quarter * (h + 1)]
        gram_ref[h] = jnp.concatenate([top, low], axis=1)
    put_gram(theirs_ref, core, parts, gram_ref)


def finish_kernel(parts, share, sketched_ref, gram_ref, e_ref, mine_ref):
    core = lax.axis_index("c")
    put_gram(mine_ref, core, parts, gram_ref)
    put_products(mine_ref, core, parts, share, sketched_ref[...], e_ref)


def begin(sketch_map, expression, parts):
    rows, genes = sketch_map.shape
    cells = expression.shape[1]
    return pl.pallas_call(
        functools.partial(begin_kernel, parts, genes // parts),
        in_specs=[pl.BlockSpec(memory_space=pltpu.HBM)] * 2,
        out_specs=[pl.BlockSpec(memory_space=pltpu.VMEM)] * 4,
        out_shape=[
            pltpu.VMEM((rows // 4, 8 * parts + rows // 4, 128), jnp.float32),
            pltpu.VMEM((rows, cells), jnp.bfloat16),
            pltpu.VMEM((2, rows // 4, 128), jnp.float32),
            pltpu.VMEM((genes, cells), jnp.bfloat16),
        ],
        scratch_shapes=[
            pltpu.VMEM((rows, genes), jnp.bfloat16),
            pltpu.VMEM((rows, max(BLOCKS)), jnp.float32),
            pltpu.SemaphoreType.DMA((len(PIECES) * len(BLOCKS) + 1,)),
        ],
        compiler_params=pltpu.CompilerParams(vmem_limit_bytes=24 << 20),
        name="begin",
    )(
        pltpu.with_memory_space_constraint(sketch_map, pltpu.HBM),
        pltpu.with_memory_space_constraint(expression, pltpu.HBM),
    )


def finish(sketched, gram, expression, parts):
    genes, cells = expression.shape
    rows = sketched.shape[0]
    return pl.pallas_call(
        functools.partial(finish_kernel, parts, genes // parts),
        in_specs=[pl.BlockSpec(memory_space=pltpu.VMEM)] * 3,
        out_specs=pl.BlockSpec(memory_space=pltpu.VMEM),
        out_shape=pltpu.VMEM((rows // 4, 8 * parts + rows // 4, 128), jnp.float32),
        cost_estimate=pl.CostEstimate(
            flops=rows * genes * cells, bytes_accessed=genes * cells * 2, transcendentals=0
        ),
        compiler_params=pltpu.CompilerParams(vmem_limit_bytes=24 << 20),
        name="finish",
    )(near(sketched), near(gram), near(expression))


def small(kernel, shape, name, *args, space=jax.ShapeDtypeStruct):
    return pl.pallas_call(
        kernel,
        in_specs=[pl.BlockSpec(memory_space=pltpu.VMEM)] * len(args),
        out_specs=pl.BlockSpec(memory_space=pltpu.VMEM),
        out_shape=space(shape, jnp.float32),
        name=name,
    )(*args)


def over_tile(x):
    return jnp.broadcast_to(x, (8, 128))


def inverse_factor(work, sub):
    count = len(work)
    for g in range(count):
        block = work[g]
        at = 64 + 8 * g
        columns = [over_tile(block[:, at + j : at + j + 1]) for j in range(8)]
        a = {(i, j): over_tile(columns[j][i : i + 1]) for j in range(8) for i in range(j, 8)}
        rows = [over_tile(block[i : i + 1]) for i in range(8)]
        low, inverse = {}, []
        for j in range(8):
            inverse.append(1.0 / a[j, j])
            for i in range(j + 1, 8):
                low[i, j] = a[i, j] * inverse[j]
            for i in range(j + 1, 8):
                for m in range(j + 1, i + 1):
                    a[i, m] = a[i, m] - low[i, j] * a[m, j]
        solved = []
        for i in range(8):
            row = rows[i]
            for j in range(i):
                row = row - low[i, j] * solved[j]
            solved.append(row)
        if g < count - 1:
            back = [None] * 8
            for i in reversed(range(8)):
                row = solved[i] * inverse[i]
                for j in range(i + 1, 8):
                    row = row - low[j, i] * back[j]
                back[i] = row
            for h in range(g + 1, count):
                left = work[h]
                for j in range(8):
                    left = left - over_tile(work[h][:, at + j : at + j + 1]) * back[j]
                work[h] = left
        block, pivots = solved[0], a[0, 0]
        for i in range(1, 8):
            block = jnp.where(sub == i, solved[i], block)
            pivots = jnp.where(sub == i, a[i, i], pivots)
        work[g] = block * lax.rsqrt(pivots)
    return work


def factor_kernel(mine_ref, other_ref, out_ref):
    me = lax.axis_index("c")
    mine, other = mine_ref[...], other_ref[...]
    halves = [jnp.where(me == 0, mine, other), jnp.where(me == 0, other, mine)]
    sub = lax.broadcasted_iota(jnp.int32, (8, 128), 0)
    lane = lax.broadcasted_iota(jnp.int32, (8, 128), 1)
    work = []
    for g in range(8):
        held = halves[g // 4][8 * (g % 2) : 8 * (g % 2) + 8]
        if g // 2 % 2 == 0:
            held = pltpu.roll(held, 64, 1)
        work.append(jnp.where(lane < 64, jnp.where(lane == sub + 8 * g, 1.0, 0.0), held))
    for g, block in enumerate(inverse_factor(work, sub)):
        out_ref[8 * g : 8 * g + 8, :] = block[:, :64]


def apply_kernel(parts, inverse_ref, in_ref, out_ref):
    rows, share = out_ref.shape
    genes = jnp.concatenate(
        [
            jnp.concatenate([in_ref[(2 * r + h) * 2 + c] for r in range(rows // 8)], axis=0)
            for c in range(2)
            for h in range(2)
        ],
        axis=1,
    )
    solved = lax.dot_general(
        inverse_ref[...],
        genes,
        (((1,), (0,)), ((), ())),
        precision=lax.Precision.HIGHEST,
        preferred_element_type=jnp.float32,
    )
    extra = lax.axis_index("z") * share % 16
    for shift in sorted({z * share % 16 for z in range(parts)}):

        @pl.when(extra == shift)
        def _():
            out_ref[...] = solved[:, shift : shift + share]


def near(x):
    return pltpu.with_memory_space_constraint(x, pltpu.VMEM)


def on_device(expression, sketch_map):
    rows, genes = sketch_map.shape
    parts = lax.axis_size("z")
    swap = [(0, 1), (1, 0)]
    theirs, sketched, gram, held = begin(sketch_map, expression, parts)
    theirs = lax.ppermute(theirs, "c", swap)
    summed = finish(sketched, gram, held, parts) + theirs
    total = lax.all_to_all(summed, ("y", "x"), 0, 0, tiled=True).sum(axis=0)
    ours = total[: 8 * parts].reshape(parts, 8, 128)
    square = jnp.broadcast_to(total[None, 8 * parts :], (parts, rows // 4, 128))
    piece = jnp.concatenate([ours, square], axis=1)
    piece = lax.all_to_all(piece, "z", 0, 0, tiled=True).sum(axis=0)
    spread = jnp.broadcast_to(piece[None, :8], (lax.axis_size(WIDE), 8, 128))
    gathered = near(lax.all_to_all(near(spread), WIDE, 0, 0, tiled=True))
    square = piece[8:]
    other = near(lax.ppermute(square, "c", swap))
    inverse = small(
        factor_kernel, (rows, rows), "factor", near(square), other, space=pltpu.VMEM
    )
    return small(
        functools.partial(apply_kernel, parts),
        (rows, genes // parts),
        "apply",
        near(inverse),
        gathered,
    )


def solution(mesh):
    grid = Mesh(mesh.devices.reshape(4, 4, 2, 8), ("y", "x", "c", "z"))
    placed = (P(None, ("y", "x", "c", "z")), P())
    return jax.shard_map(
        on_device, mesh=grid, in_specs=placed, out_specs=P(None, "z"), check_vma=False
    )
```

```python
import functools

import jax
import jax.numpy as jnp
from jax import lax
from jax.experimental import pallas as pl
from jax.experimental.pallas import tpu as pltpu
from jax.sharding import PartitionSpec as P

PIECES = (1024, 1024, 1024, 928)
BLOCKS = (512, 512, 512)
SPAN = 256


def nn(a, b):
    return lax.dot_general(a, b, (((1,), (0,)), ((), ())), preferred_element_type=jnp.float32)


def nt(a, b):
    return lax.dot_general(a, b, (((1,), (1,)), ((), ())), preferred_element_type=jnp.float32)


def window_start(z, share):
    return z * share // 16 * 16


def place():
    index = lax.axis_index("wide")
    core, x, y = index & 1, (index >> 1) & 3, index >> 3
    along_x, along_y = (x ^ (x >> 1)) & 1, (y ^ (y >> 1)) & 1
    return core, jnp.where(core == 0, along_x, along_y), jnp.where(core == 0, along_y, along_x)


def put_products(ref, core, parts, share, sketched, e_ref, cells=slice(None), add=False):
    rows = sketched.shape[0]
    for z in range(parts):
        start = pl.multiple_of(window_start(z, share) + SPAN * core, 16)
        part = nt(sketched, e_ref[pl.ds(start, SPAN), cells])
        for t in range(2):
            tile = part[:, 128 * t : 128 * t + 128]
            if add:
                tile = ref[t, rows * z : rows * z + rows, :] + tile
            ref[t, rows * z : rows * z + rows, :] = tile


def put_gram(ref, core, parts, gram_ref):
    half = gram_ref[core]
    for t in range(2):
        ref[t, ref.shape[1] - half.shape[0] :, :] = half


def begin_kernel(parts, share, s_hbm, e_hbm, theirs_ref, sketched_ref, gram_ref, e_ref, *scratch):
    s_ref, acc, sems = scratch
    count = len(PIECES)
    spans = [slice(sum(PIECES[:i]), sum(PIECES[: i + 1])) for i in range(count)]
    blocks = [slice(sum(BLOCKS[:j]), sum(BLOCKS[: j + 1])) for j in range(len(BLOCKS))]
    whole = pltpu.make_async_copy(s_hbm, s_ref, sems.at[count * len(BLOCKS)])
    whole.start()
    copies = []
    for j, block in enumerate(blocks):
        for i, span in enumerate(spans):
            where = (pl.ds(span.start, PIECES[i]), pl.ds(block.start, BLOCKS[j]))
            copy = pltpu.make_async_copy(e_hbm.at[where], e_ref.at[where], sems.at[j * count + i])
            copy.start()
            copies.append(copy)
    whole.wait()
    core = 1 - place()[0]
    square = None
    for j, block in enumerate(blocks):
        for i, span in enumerate(spans):
            copies[j * count + i].wait()
            term = nn(s_ref[:, span], e_ref[span, block])
            if i > 0:
                term = acc[:, : BLOCKS[j]] + term
            if i < count - 1:
                acc[:, : BLOCKS[j]] = term
        sketched = term.astype(jnp.bfloat16)
        sketched_ref[:, block] = sketched
        term = nt(sketched, sketched)
        square = term if j == 0 else square + term
        put_products(theirs_ref, core, parts, share, sketched, e_ref, block, j > 0)
    quarter = square.shape[0] // 4
    for h in range(2):
        top = square[2 * quarter * h : 2 * quarter * h + quarter]
        low = square[2 * quarter * h + quarter : 2 * quarter * (h + 1)]
        gram_ref[h] = jnp.concatenate([top, low], axis=1)
    put_gram(theirs_ref, core, parts, gram_ref)


def finish_kernel(parts, share, sketched_ref, gram_ref, e_ref, mine_ref):
    core = place()[0]
    put_gram(mine_ref, core, parts, gram_ref)
    put_products(mine_ref, core, parts, share, sketched_ref[...], e_ref)


def begin(sketch_map, expression, parts):
    rows, genes = sketch_map.shape
    cells = expression.shape[1]
    return pl.pallas_call(
        functools.partial(begin_kernel, parts, genes // parts),
        in_specs=[pl.BlockSpec(memory_space=pltpu.HBM)] * 2,
        out_specs=[pl.BlockSpec(memory_space=pltpu.VMEM)] * 4,
        out_shape=[
            pltpu.VMEM((2, rows * parts + rows // 4, 128), jnp.float32),
            pltpu.VMEM((rows, cells), jnp.bfloat16),
            pltpu.VMEM((2, rows // 4, 128), jnp.float32),
            pltpu.VMEM((genes, cells), jnp.bfloat16),
        ],
        scratch_shapes=[
            pltpu.VMEM((rows, genes), jnp.bfloat16),
            pltpu.VMEM((rows, max(BLOCKS)), jnp.float32),
            pltpu.SemaphoreType.DMA((len(PIECES) * len(BLOCKS) + 1,)),
        ],
        compiler_params=pltpu.CompilerParams(vmem_limit_bytes=16 << 20),
        name="begin",
    )(
        pltpu.with_memory_space_constraint(sketch_map, pltpu.HBM),
        pltpu.with_memory_space_constraint(expression, pltpu.HBM),
    )


def finish(sketched, gram, expression, parts):
    genes, cells = expression.shape
    rows = sketched.shape[0]
    return pl.pallas_call(
        functools.partial(finish_kernel, parts, genes // parts),
        in_specs=[pl.BlockSpec(memory_space=pltpu.VMEM)] * 3,
        out_specs=pl.BlockSpec(memory_space=pltpu.VMEM),
        out_shape=pltpu.VMEM((2, rows * parts + rows // 4, 128), jnp.float32),
        cost_estimate=pl.CostEstimate(
            flops=rows * genes * cells, bytes_accessed=genes * cells * 2, transcendentals=0
        ),
        compiler_params=pltpu.CompilerParams(vmem_limit_bytes=8 << 20),
        name="finish",
    )(near(sketched), near(gram), near(expression))


def small(kernel, shape, name, *args, space=jax.ShapeDtypeStruct):
    return pl.pallas_call(
        kernel,
        in_specs=[pl.BlockSpec(memory_space=pltpu.VMEM)] * len(args),
        out_specs=pl.BlockSpec(memory_space=pltpu.VMEM),
        out_shape=space(shape, jnp.float32),
        name=name,
    )(*args)


def over_tile(x):
    return jnp.broadcast_to(x, (8, 128))


def inverse_factor(work, sub):
    count = len(work)
    for g in range(count):
        block = work[g]
        at = 64 + 8 * g
        columns = [over_tile(block[:, at + j : at + j + 1]) for j in range(8)]
        a = {(i, j): over_tile(columns[j][i : i + 1]) for j in range(8) for i in range(j, 8)}
        rows = [over_tile(block[i : i + 1]) for i in range(8)]
        low, inverse = {}, []
        for j in range(8):
            inverse.append(1.0 / a[j, j])
            for i in range(j + 1, 8):
                low[i, j] = a[i, j] * inverse[j]
            for i in range(j + 1, 8):
                for m in range(j + 1, i + 1):
                    a[i, m] = a[i, m] - low[i, j] * a[m, j]
        solved = []
        for i in range(8):
            row = rows[i]
            for j in range(i):
                row = row - low[i, j] * solved[j]
            solved.append(row)
        if g < count - 1:
            back = [None] * 8
            for i in reversed(range(8)):
                row = solved[i] * inverse[i]
                for j in range(i + 1, 8):
                    row = row - low[j, i] * back[j]
                back[i] = row
            for h in range(g + 1, count):
                left = work[h]
                for j in range(8):
                    left = left - over_tile(work[h][:, at + j : at + j + 1]) * back[j]
                work[h] = left
        block, pivots = solved[0], a[0, 0]
        for i in range(1, 8):
            block = jnp.where(sub == i, solved[i], block)
            pivots = jnp.where(sub == i, a[i, i], pivots)
        work[g] = block * lax.rsqrt(pivots)
    return work


def factor_kernel(mine_ref, other_ref, out_ref):
    me = place()[0]
    mine, other = mine_ref[...], other_ref[...]
    halves = [jnp.where(me == 0, mine, other), jnp.where(me == 0, other, mine)]
    sub = lax.broadcasted_iota(jnp.int32, (8, 128), 0)
    lane = lax.broadcasted_iota(jnp.int32, (8, 128), 1)
    work = []
    for g in range(8):
        held = halves[g // 4][8 * (g % 2) : 8 * (g % 2) + 8]
        if g // 2 % 2 == 0:
            held = pltpu.roll(held, 64, 1)
        work.append(jnp.where(lane < 64, jnp.where(lane == sub + 8 * g, 1.0, 0.0), held))
    for g, block in enumerate(inverse_factor(work, sub)):
        out_ref[8 * g : 8 * g + 8, :] = block[:, :64]


def apply_kernel(parts, inverse_ref, mine_ref, other_ref, out_ref):
    rows, share = out_ref.shape
    core, kept, across = place()
    mine = [mine_ref[:rows], mine_ref[rows:]]
    other = [other_ref[:rows], other_ref[rows:]]
    mine = [jnp.where(kept == t, mine[0], mine[1]) for t in range(2)]
    other = [jnp.where(across == t, other[0], other[1]) for t in range(2)]
    tiles = [jnp.where(core == 0, p, q) for p, q in zip(mine + other, other + mine)]
    solved = lax.dot_general(
        inverse_ref[...],
        jnp.concatenate(tiles, axis=1),
        (((1,), (0,)), ((), ())),
        precision=lax.Precision.HIGHEST,
        preferred_element_type=jnp.float32,
    )
    extra = lax.axis_index("narrow") * share % 16
    for shift in sorted({z * share % 16 for z in range(parts)}):

        @pl.when(extra == shift)
        def _():
            out_ref[...] = solved[:, shift : shift + share]


def near(x):
    return pltpu.with_memory_space_constraint(x, pltpu.VMEM)


def wide_index(y, x, core):
    return (y * 4 + x) * 2 + core


def neighbours():
    return [
        (wide_index(y, x, core), wide_index(y ^ core, x ^ 1 ^ core, core))
        for y in range(4)
        for x in range(4)
        for core in range(2)
    ]


def holders():
    return [
        [wide_index(*((v, u) if core == 0 else (u, v)), core) for v in range(4) for u in (a, 3 - a)]
        for core in range(2)
        for a in range(2)
    ]


def on_device(expression, sketch_map):
    rows, genes = sketch_map.shape
    parts = lax.axis_size("narrow")
    swap = [(i, i ^ 1) for i in range(lax.axis_size("wide"))]
    pairs, groups = neighbours(), holders()
    kept = place()[1]
    kept, given, sketch_map = lax.optimization_barrier((kept, 1 - kept, sketch_map))
    theirs, sketched, gram, held = begin(sketch_map, expression, parts)
    theirs = lax.ppermute(theirs, "wide", swap)
    summed = finish(sketched, gram, held, parts) + theirs
    keep = lax.dynamic_slice_in_dim(summed, kept, 1, 0, allow_negative_indices=False)[0]
    give = lax.dynamic_slice_in_dim(summed, given, 1, 0, allow_negative_indices=False)[0]
    half = keep + lax.ppermute(give, "wide", pairs)
    ours = half[: rows * parts].reshape(parts, rows, 128)
    square = jnp.broadcast_to(half[None, rows * parts :], (parts, rows // 4, 128))
    piece = jnp.concatenate([ours, square], axis=1)
    piece = lax.all_to_all(piece, "narrow", 0, 0, tiled=True).sum(axis=0)
    spread = jnp.broadcast_to(piece[None], (len(groups[0]), *piece.shape))
    spread = lax.all_to_all(spread, "wide", 0, 0, axis_index_groups=groups, tiled=True)
    total = spread.sum(axis=0)
    ours, square = total[:rows], total[rows:]
    beside = lax.ppermute(ours, "wide", pairs)
    inverse = small(
        factor_kernel,
        (rows, rows),
        "factor",
        near(square),
        near(lax.ppermute(square, "wide", swap)),
        space=pltpu.VMEM,
    )
    beside, inverse = lax.optimization_barrier((beside, inverse))
    mine = jnp.concatenate([ours, beside], axis=0)
    other = near(lax.ppermute(mine, "wide", swap))
    return small(
        functools.partial(apply_kernel, parts),
        (rows, genes // parts),
        "apply",
        near(inverse),
        near(mine),
        other,
    )


def solution(mesh):
    placed = (P(None, ("wide", "narrow")), P())
    return jax.shard_map(
        on_device, mesh=mesh, in_specs=placed, out_specs=P(None, "narrow"), check_vma=False
    )
```

```python
import functools

import jax
import jax.numpy as jnp
from jax import lax
from jax.experimental import pallas as pl
from jax.experimental.pallas import tpu as pltpu
from jax.sharding import PartitionSpec as P

PIECES = (1024, 1024, 1024, 928)
BLOCKS = (512, 512, 512)
SPAN = 256


def nn(a, b):
    return lax.dot_general(a, b, (((1,), (0,)), ((), ())), preferred_element_type=jnp.float32)


def nt(a, b):
    return lax.dot_general(a, b, (((1,), (1,)), ((), ())), preferred_element_type=jnp.float32)


def window_start(z, share):
    return z * share // 16 * 16


def place():
    index = lax.axis_index("wide")
    core, x, y = index & 1, (index >> 1) & 3, index >> 3
    along_x, along_y = (x ^ (x >> 1)) & 1, (y ^ (y >> 1)) & 1
    return core, jnp.where(core == 0, along_x, along_y), jnp.where(core == 0, along_y, along_x)


def put_products(ref, core, half, parts, share, sketched, e_ref, cells=slice(None), add=False):
    rows = sketched.shape[0]
    for z in range(parts):
        start = pl.multiple_of(window_start(z, share) + SPAN * core + SPAN // 2 * half, 16)
        tile = nt(sketched, e_ref[pl.ds(start, SPAN // 2), cells])
        if add:
            tile = ref[rows * z : rows * z + rows, :] + tile
        ref[rows * z : rows * z + rows, :] = tile


def put_gram(ref, core, gram_ref):
    half = gram_ref[core]
    ref[ref.shape[0] - half.shape[0] :, :] = half


def begin_kernel(parts, share, s_hbm, e_hbm, theirs_ref, sketched_ref, gram_ref, e_ref, *scratch):
    s_ref, acc, sems = scratch
    count = len(PIECES)
    spans = [slice(sum(PIECES[:i]), sum(PIECES[: i + 1])) for i in range(count)]
    blocks = [slice(sum(BLOCKS[:j]), sum(BLOCKS[: j + 1])) for j in range(len(BLOCKS))]
    whole = pltpu.make_async_copy(s_hbm, s_ref, sems.at[count * len(BLOCKS)])
    whole.start()
    copies = []
    for j, block in enumerate(blocks):
        for i, span in enumerate(spans):
            where = (pl.ds(span.start, PIECES[i]), pl.ds(block.start, BLOCKS[j]))
            copy = pltpu.make_async_copy(e_hbm.at[where], e_ref.at[where], sems.at[j * count + i])
            copy.start()
            copies.append(copy)
    whole.wait()
    core, _, half = place()
    core, half = 1 - core, 1 - half
    square = None
    for j, block in enumerate(blocks):
        for i, span in enumerate(spans):
            copies[j * count + i].wait()
            term = nn(s_ref[:, span], e_ref[span, block])
            if i > 0:
                term = acc[:, : BLOCKS[j]] + term
            if i < count - 1:
                acc[:, : BLOCKS[j]] = term
        sketched = term.astype(jnp.bfloat16)
        sketched_ref[:, block] = sketched
        term = nt(sketched, sketched)
        square = term if j == 0 else square + term
        put_products(theirs_ref, core, half, parts, share, sketched, e_ref, block, j > 0)
    quarter = square.shape[0] // 4
    for h in range(2):
        top = square[2 * quarter * h : 2 * quarter * h + quarter]
        low = square[2 * quarter * h + quarter : 2 * quarter * (h + 1)]
        gram_ref[h] = jnp.concatenate([top, low], axis=1)
    put_gram(theirs_ref, core, gram_ref)


def more_kernel(which, parts, share, sketched_ref, gram_ref, e_ref, out_ref):
    core, kept, across = place()
    core, half = {"give": (core, 1 - kept), "keep": (core, kept), "theirs": (1 - core, across)}[which]
    put_gram(out_ref, core, gram_ref)
    put_products(out_ref, core, half, parts, share, sketched_ref[...], e_ref)


def begin(sketch_map, expression, parts):
    rows, genes = sketch_map.shape
    cells = expression.shape[1]
    return pl.pallas_call(
        functools.partial(begin_kernel, parts, genes // parts),
        in_specs=[pl.BlockSpec(memory_space=pltpu.HBM)] * 2,
        out_specs=[pl.BlockSpec(memory_space=pltpu.VMEM)] * 4,
        out_shape=[
            pltpu.VMEM((rows * parts + rows // 4, 128), jnp.float32),
            pltpu.VMEM((rows, cells), jnp.bfloat16),
            pltpu.VMEM((2, rows // 4, 128), jnp.float32),
            pltpu.VMEM((genes, cells), jnp.bfloat16),
        ],
        scratch_shapes=[
            pltpu.VMEM((rows, genes), jnp.bfloat16),
            pltpu.VMEM((rows, max(BLOCKS)), jnp.float32),
            pltpu.SemaphoreType.DMA((len(PIECES) * len(BLOCKS) + 1,)),
        ],
        compiler_params=pltpu.CompilerParams(vmem_limit_bytes=16 << 20),
        name="begin",
    )(
        pltpu.with_memory_space_constraint(sketch_map, pltpu.HBM),
        pltpu.with_memory_space_constraint(expression, pltpu.HBM),
    )


def more(which, sketched, gram, expression, parts):
    genes, cells = expression.shape
    rows = sketched.shape[0]
    return pl.pallas_call(
        functools.partial(more_kernel, which, parts, genes // parts),
        in_specs=[pl.BlockSpec(memory_space=pltpu.VMEM)] * 3,
        out_specs=pl.BlockSpec(memory_space=pltpu.VMEM),
        out_shape=pltpu.VMEM((rows * parts + rows // 4, 128), jnp.float32),
        cost_estimate=pl.CostEstimate(
            flops=rows * genes * cells // 2, bytes_accessed=genes * cells, transcendentals=0
        ),
        compiler_params=pltpu.CompilerParams(vmem_limit_bytes=8 << 20),
        name=which,
    )(near(sketched), near(gram), near(expression))


def small(kernel, shape, name, *args, space=jax.ShapeDtypeStruct):
    return pl.pallas_call(
        kernel,
        in_specs=[pl.BlockSpec(memory_space=pltpu.VMEM)] * len(args),
        out_specs=pl.BlockSpec(memory_space=pltpu.VMEM),
        out_shape=space(shape, jnp.float32),
        name=name,
    )(*args)


def over_tile(x):
    return jnp.broadcast_to(x, (8, 128))


def inverse_factor(work, sub):
    count = len(work)
    for g in range(count):
        block = work[g]
        at = 64 + 8 * g
        columns = [over_tile(block[:, at + j : at + j + 1]) for j in range(8)]
        a = {(i, j): over_tile(columns[j][i : i + 1]) for j in range(8) for i in range(j, 8)}
        rows = [over_tile(block[i : i + 1]) for i in range(8)]
        low, inverse = {}, []
        for j in range(8):
            inverse.append(1.0 / a[j, j])
            for i in range(j + 1, 8):
                low[i, j] = a[i, j] * inverse[j]
            for i in range(j + 1, 8):
                for m in range(j + 1, i + 1):
                    a[i, m] = a[i, m] - low[i, j] * a[m, j]
        solved = []
        for i in range(8):
            row = rows[i]
            for j in range(i):
                row = row - low[i, j] * solved[j]
            solved.append(row)
        if g < count - 1:
            back = [None] * 8
            for i in reversed(range(8)):
                row = solved[i] * inverse[i]
                for j in range(i + 1, 8):
                    row = row - low[j, i] * back[j]
                back[i] = row
            for h in range(g + 1, count):
                left = work[h]
                for j in range(8):
                    left = left - over_tile(work[h][:, at + j : at + j + 1]) * back[j]
                work[h] = left
        block, pivots = solved[0], a[0, 0]
        for i in range(1, 8):
            block = jnp.where(sub == i, solved[i], block)
            pivots = jnp.where(sub == i, a[i, i], pivots)
        work[g] = block * lax.rsqrt(pivots)
    return work


def factor_kernel(mine_ref, other_ref, out_ref):
    me = place()[0]
    mine, other = mine_ref[...], other_ref[...]
    halves = [jnp.where(me == 0, mine, other), jnp.where(me == 0, other, mine)]
    sub = lax.broadcasted_iota(jnp.int32, (8, 128), 0)
    lane = lax.broadcasted_iota(jnp.int32, (8, 128), 1)
    work = []
    for g in range(8):
        held = halves[g // 4][8 * (g % 2) : 8 * (g % 2) + 8]
        if g // 2 % 2 == 0:
            held = pltpu.roll(held, 64, 1)
        work.append(jnp.where(lane < 64, jnp.where(lane == sub + 8 * g, 1.0, 0.0), held))
    for g, block in enumerate(inverse_factor(work, sub)):
        out_ref[8 * g : 8 * g + 8, :] = block[:, :64]


def apply_kernel(parts, inverse_ref, mine_ref, other_ref, out_ref):
    rows, share = out_ref.shape
    core, kept, across = place()
    mine = [mine_ref[:rows], mine_ref[rows:]]
    other = [other_ref[:rows], other_ref[rows:]]
    mine = [jnp.where(kept == t, mine[0], mine[1]) for t in range(2)]
    other = [jnp.where(across == t, other[0], other[1]) for t in range(2)]
    tiles = [jnp.where(core == 0, p, q) for p, q in zip(mine + other, other + mine)]
    solved = lax.dot_general(
        inverse_ref[...],
        jnp.concatenate(tiles, axis=1),
        (((1,), (0,)), ((), ())),
        precision=lax.Precision.HIGHEST,
        preferred_element_type=jnp.float32,
    )
    extra = lax.axis_index("narrow") * share % 16
    for shift in sorted({z * share % 16 for z in range(parts)}):

        @pl.when(extra == shift)
        def _():
            out_ref[...] = solved[:, shift : shift + share]


def near(x):
    return pltpu.with_memory_space_constraint(x, pltpu.VMEM)


def wide_index(y, x, core):
    return (y * 4 + x) * 2 + core


def neighbours():
    return [
        (wide_index(y, x, core), wide_index(y ^ core, x ^ 1 ^ core, core))
        for y in range(4)
        for x in range(4)
        for core in range(2)
    ]


def holders():
    return [
        [wide_index(*((v, u) if core == 0 else (u, v)), core) for v in range(4) for u in (a, 3 - a)]
        for core in range(2)
        for a in range(2)
    ]


def on_device(expression, sketch_map):
    rows, genes = sketch_map.shape
    parts = lax.axis_size("narrow")
    swap = [(i, i ^ 1) for i in range(lax.axis_size("wide"))]
    pairs, groups = neighbours(), holders()
    theirs, sketched, gram, held = begin(sketch_map, expression, parts)
    theirs = lax.ppermute(theirs, "wide", swap)
    give = more("give", sketched, gram, held, parts) + theirs
    give, gram = lax.optimization_barrier((give, gram))
    given = lax.ppermute(give, "wide", pairs)
    theirs = lax.ppermute(more("theirs", sketched, gram, held, parts), "wide", swap)
    half = more("keep", sketched, gram, held, parts) + theirs + given
    ours = half[: rows * parts].reshape(parts, rows, 128)
    square = jnp.broadcast_to(half[None, rows * parts :], (parts, rows // 4, 128))
    piece = jnp.concatenate([ours, square], axis=1)
    piece = lax.all_to_all(piece, "narrow", 0, 0, tiled=True).sum(axis=0)
    spread = jnp.broadcast_to(piece[None], (len(groups[0]), *piece.shape))
    spread = lax.all_to_all(spread, "wide", 0, 0, axis_index_groups=groups, tiled=True)
    total = spread.sum(axis=0)
    ours, square = total[:rows], total[rows:]
    beside = lax.ppermute(ours, "wide", pairs)
    inverse = small(
        factor_kernel,
        (rows, rows),
        "factor",
        near(square),
        near(lax.ppermute(square, "wide", swap)),
        space=pltpu.VMEM,
    )
    beside, inverse = lax.optimization_barrier((beside, inverse))
    mine = jnp.concatenate([ours, beside], axis=0)
    other = near(lax.ppermute(mine, "wide", swap))
    return small(
        functools.partial(apply_kernel, parts),
        (rows, genes // parts),
        "apply",
        near(inverse),
        near(mine),
        other,
    )


def solution(mesh):
    placed = (P(None, ("wide", "narrow")), P())
    return jax.shard_map(
        on_device, mesh=mesh, in_specs=placed, out_specs=P(None, "narrow"), check_vma=False
    )
```

```python
import functools

import jax
import jax.numpy as jnp
from jax import lax
from jax.experimental import pallas as pl
from jax.experimental.pallas import tpu as pltpu
from jax.sharding import PartitionSpec as P

PIECES = (1024, 1024, 1024, 928)
BLOCKS = (512, 512, 512)
SPAN = 256


def nn(a, b):
    return lax.dot_general(a, b, (((1,), (0,)), ((), ())), preferred_element_type=jnp.float32)


def nt(a, b):
    return lax.dot_general(a, b, (((1,), (1,)), ((), ())), preferred_element_type=jnp.float32)


def window_start(z, share):
    return z * share // 16 * 16


def place():
    index = lax.axis_index("wide")
    core, x, y = index & 1, (index >> 1) & 3, index >> 3
    along_x, along_y = (x ^ (x >> 1)) & 1, (y ^ (y >> 1)) & 1
    return core, jnp.where(core == 0, along_x, along_y), jnp.where(core == 0, along_y, along_x)


def put_products(ref, core, half, parts, share, sketched, e_ref, cells=slice(None), add=False):
    rows = sketched.shape[0]
    for z in range(parts):
        start = pl.multiple_of(window_start(z, share) + SPAN * core + SPAN // 2 * half, 16)
        tile = nt(sketched, e_ref[pl.ds(start, SPAN // 2), cells])
        if add:
            tile = ref[rows * z : rows * z + rows, :] + tile
        ref[rows * z : rows * z + rows, :] = tile


def put_gram(ref, core, gram_ref):
    half = gram_ref[core]
    ref[ref.shape[0] - half.shape[0] :, :] = half


def begin_kernel(parts, share, s_hbm, e_hbm, theirs_ref, sketched_ref, gram_ref, e_ref, *scratch):
    s_ref, acc, sems = scratch
    count = len(PIECES)
    spans = [slice(sum(PIECES[:i]), sum(PIECES[: i + 1])) for i in range(count)]
    blocks = [slice(sum(BLOCKS[:j]), sum(BLOCKS[: j + 1])) for j in range(len(BLOCKS))]
    whole = pltpu.make_async_copy(s_hbm, s_ref, sems.at[count * len(BLOCKS)])
    whole.start()
    copies = []
    for j, block in enumerate(blocks):
        for i, span in enumerate(spans):
            where = (pl.ds(span.start, PIECES[i]), pl.ds(block.start, BLOCKS[j]))
            copy = pltpu.make_async_copy(e_hbm.at[where], e_ref.at[where], sems.at[j * count + i])
            copy.start()
            copies.append(copy)
    whole.wait()
    core, _, half = place()
    core, half = 1 - core, 1 - half
    square = None
    for j, block in enumerate(blocks):
        for i, span in enumerate(spans):
            copies[j * count + i].wait()
            term = nn(s_ref[:, span], e_ref[span, block])
            if i > 0:
                term = acc[:, : BLOCKS[j]] + term
            if i < count - 1:
                acc[:, : BLOCKS[j]] = term
        sketched = term.astype(jnp.bfloat16)
        sketched_ref[:, block] = sketched
        term = nt(sketched, sketched)
        square = term if j == 0 else square + term
        put_products(theirs_ref, core, half, parts, share, sketched, e_ref, block, j > 0)
    quarter = square.shape[0] // 4
    for h in range(2):
        top = square[2 * quarter * h : 2 * quarter * h + quarter]
        low = square[2 * quarter * h + quarter : 2 * quarter * (h + 1)]
        gram_ref[h] = jnp.concatenate([top, low], axis=1)
    put_gram(theirs_ref, core, gram_ref)


def more_kernel(which, parts, share, sketched_ref, gram_ref, e_ref, out_ref):
    core, kept, across = place()
    core, half = {"give": (core, 1 - kept), "keep": (core, kept), "theirs": (1 - core, across)}[which]
    put_gram(out_ref, core, gram_ref)
    put_products(out_ref, core, half, parts, share, sketched_ref[...], e_ref)


def begin(sketch_map, expression, parts):
    rows, genes = sketch_map.shape
    cells = expression.shape[1]
    return pl.pallas_call(
        functools.partial(begin_kernel, parts, genes // parts),
        in_specs=[pl.BlockSpec(memory_space=pltpu.HBM)] * 2,
        out_specs=[pl.BlockSpec(memory_space=pltpu.VMEM)] * 4,
        out_shape=[
            pltpu.VMEM((rows * parts + rows // 4, 128), jnp.float32),
            pltpu.VMEM((rows, cells), jnp.bfloat16),
            pltpu.VMEM((2, rows // 4, 128), jnp.float32),
            pltpu.VMEM((genes, cells), jnp.bfloat16),
        ],
        scratch_shapes=[
            pltpu.VMEM((rows, genes), jnp.bfloat16),
            pltpu.VMEM((rows, max(BLOCKS)), jnp.float32),
            pltpu.SemaphoreType.DMA((len(PIECES) * len(BLOCKS) + 1,)),
        ],
        compiler_params=pltpu.CompilerParams(vmem_limit_bytes=16 << 20),
        name="begin",
    )(
        pltpu.with_memory_space_constraint(sketch_map, pltpu.HBM),
        pltpu.with_memory_space_constraint(expression, pltpu.HBM),
    )


def more(which, sketched, gram, expression, parts):
    genes, cells = expression.shape
    rows = sketched.shape[0]
    return pl.pallas_call(
        functools.partial(more_kernel, which, parts, genes // parts),
        in_specs=[pl.BlockSpec(memory_space=pltpu.VMEM)] * 3,
        out_specs=pl.BlockSpec(memory_space=pltpu.VMEM),
        out_shape=pltpu.VMEM((rows * parts + rows // 4, 128), jnp.float32),
        cost_estimate=pl.CostEstimate(
            flops=rows * genes * cells // 2, bytes_accessed=genes * cells, transcendentals=0
        ),
        compiler_params=pltpu.CompilerParams(vmem_limit_bytes=8 << 20),
        name=which,
    )(near(sketched), near(gram), near(expression))


def small(kernel, shape, name, *args, space=jax.ShapeDtypeStruct):
    return pl.pallas_call(
        kernel,
        in_specs=[pl.BlockSpec(memory_space=pltpu.VMEM)] * len(args),
        out_specs=pl.BlockSpec(memory_space=pltpu.VMEM),
        out_shape=space(shape, jnp.float32),
        name=name,
    )(*args)


def over_tile(x):
    return jnp.broadcast_to(x, (8, 128))


def inverse_factor(work, sub):
    count = len(work)
    for g in range(count):
        block = work[g]
        at = 64 + 8 * g
        columns = [over_tile(block[:, at + j : at + j + 1]) for j in range(8)]
        a = {(i, j): over_tile(columns[j][i : i + 1]) for j in range(8) for i in range(j, 8)}
        rows = [over_tile(block[i : i + 1]) for i in range(8)]
        low, inverse = {}, []
        for j in range(8):
            inverse.append(1.0 / a[j, j])
            for i in range(j + 1, 8):
                low[i, j] = a[i, j] * inverse[j]
            for i in range(j + 1, 8):
                for m in range(j + 1, i + 1):
                    a[i, m] = a[i, m] - low[i, j] * a[m, j]
        solved = []
        for i in range(8):
            row = rows[i]
            for j in range(i):
                row = row - low[i, j] * solved[j]
            solved.append(row)
        if g < count - 1:
            back = [None] * 8
            for i in reversed(range(8)):
                row = solved[i] * inverse[i]
                for j in range(i + 1, 8):
                    row = row - low[j, i] * back[j]
                back[i] = row
            for h in range(g + 1, count):
                left = work[h]
                for j in range(8):
                    left = left - over_tile(work[h][:, at + j : at + j + 1]) * back[j]
                work[h] = left
        block, pivots = solved[0], a[0, 0]
        for i in range(1, 8):
            block = jnp.where(sub == i, solved[i], block)
            pivots = jnp.where(sub == i, a[i, i], pivots)
        work[g] = block * lax.rsqrt(pivots)
    return work


def factor_kernel(mine_ref, other_ref, out_ref):
    me = place()[0]
    mine, other = mine_ref[...], other_ref[...]
    halves = [jnp.where(me == 0, mine, other), jnp.where(me == 0, other, mine)]
    sub = lax.broadcasted_iota(jnp.int32, (8, 128), 0)
    lane = lax.broadcasted_iota(jnp.int32, (8, 128), 1)
    work = []
    for g in range(8):
        held = halves[g // 4][8 * (g % 2) : 8 * (g % 2) + 8]
        if g // 2 % 2 == 0:
            held = pltpu.roll(held, 64, 1)
        work.append(jnp.where(lane < 64, jnp.where(lane == sub + 8 * g, 1.0, 0.0), held))
    for g, block in enumerate(inverse_factor(work, sub)):
        out_ref[8 * g : 8 * g + 8, :] = block[:, :64]


def apply_kernel(parts, inverse_ref, mine_ref, other_ref, out_ref):
    rows, share = out_ref.shape
    core, kept, across = place()
    mine = [mine_ref[:rows], mine_ref[rows:]]
    other = [other_ref[:rows], other_ref[rows:]]
    mine = [jnp.where(kept == t, mine[0], mine[1]) for t in range(2)]
    other = [jnp.where(across == t, other[0], other[1]) for t in range(2)]
    tiles = [jnp.where(core == 0, p, q) for p, q in zip(mine + other, other + mine)]
    solved = lax.dot_general(
        inverse_ref[...],
        jnp.concatenate(tiles, axis=1),
        (((1,), (0,)), ((), ())),
        precision=lax.Precision.HIGHEST,
        preferred_element_type=jnp.float32,
    )
    extra = lax.axis_index("narrow") * share % 16
    for shift in sorted({z * share % 16 for z in range(parts)}):

        @pl.when(extra == shift)
        def _():
            out_ref[...] = solved[:, shift : shift + share]


def near(x):
    return pltpu.with_memory_space_constraint(x, pltpu.VMEM)


def wide_index(y, x, core):
    return (y * 4 + x) * 2 + core


def neighbours():
    return [
        (wide_index(y, x, core), wide_index(y ^ core, x ^ 1 ^ core, core))
        for y in range(4)
        for x in range(4)
        for core in range(2)
    ]


def holders():
    return [
        [wide_index(*((v, u) if core == 0 else (u, v)), core) for v in range(4) for u in (a, 3 - a)]
        for core in range(2)
        for a in range(2)
    ]


def on_device(expression, sketch_map):
    rows, genes = sketch_map.shape
    parts = lax.axis_size("narrow")
    swap = [(i, i ^ 1) for i in range(lax.axis_size("wide"))]
    pairs, groups = neighbours(), holders()
    theirs, sketched, gram, held = begin(sketch_map, expression, parts)
    theirs = lax.ppermute(theirs, "wide", swap)
    give = more("give", sketched, gram, held, parts) + theirs
    give, gram = lax.optimization_barrier((give, gram))
    given = lax.ppermute(give, "wide", pairs)
    theirs = lax.ppermute(more("theirs", sketched, gram, held, parts), "wide", swap)
    keep = lax.optimization_barrier(more("keep", sketched, gram, held, parts) + given)
    half = keep + theirs
    ours = half[: rows * parts].reshape(parts, rows, 128)
    square = jnp.broadcast_to(half[None, rows * parts :], (parts, rows // 4, 128))
    piece = jnp.concatenate([ours, square], axis=1)
    piece = lax.all_to_all(piece, "narrow", 0, 0, tiled=True).sum(axis=0)
    spread = jnp.broadcast_to(piece[None], (len(groups[0]), *piece.shape))
    spread = lax.all_to_all(spread, "wide", 0, 0, axis_index_groups=groups, tiled=True)
    total = spread.sum(axis=0)
    ours, square = total[:rows], total[rows:]
    beside = lax.ppermute(ours, "wide", pairs)
    inverse = small(
        factor_kernel,
        (rows, rows),
        "factor",
        near(square),
        near(lax.ppermute(square, "wide", swap)),
        space=pltpu.VMEM,
    )
    beside, inverse = lax.optimization_barrier((beside, inverse))
    mine = jnp.concatenate([ours, beside], axis=0)
    other = near(lax.ppermute(mine, "wide", swap))
    return small(
        functools.partial(apply_kernel, parts),
        (rows, genes // parts),
        "apply",
        near(inverse),
        near(mine),
        other,
    )


def solution(mesh):
    placed = (P(None, ("wide", "narrow")), P())
    return jax.shard_map(
        on_device, mesh=mesh, in_specs=placed, out_specs=P(None, "narrow"), check_vma=False
    )
```

```python
import functools

import jax
import jax.numpy as jnp
from jax import lax
from jax.experimental import pallas as pl
from jax.experimental.pallas import tpu as pltpu
from jax.sharding import PartitionSpec as P

PIECES = (1024, 1024, 1024, 928)
BLOCKS = (512, 512, 512)
SPAN = 256


def nn(a, b):
    return lax.dot_general(a, b, (((1,), (0,)), ((), ())), preferred_element_type=jnp.float32)


def nt(a, b):
    return lax.dot_general(a, b, (((1,), (1,)), ((), ())), preferred_element_type=jnp.float32)


def window_start(z, share):
    return z * share // 16 * 16


def place():
    index = lax.axis_index("wide")
    core, x, y = index & 1, (index >> 1) & 3, index >> 3
    along_x, along_y = (x ^ (x >> 1)) & 1, (y ^ (y >> 1)) & 1
    return core, jnp.where(core == 0, along_x, along_y), jnp.where(core == 0, along_y, along_x)


def put_products(ref, core, half, parts, share, sketched, e_ref, cells=slice(None), add=False):
    rows = sketched.shape[0]
    for z in range(parts):
        start = pl.multiple_of(window_start(z, share) + SPAN * core + SPAN // 2 * half, 16)
        tile = nt(sketched, e_ref[pl.ds(start, SPAN // 2), cells])
        if add:
            tile = ref[rows * z : rows * z + rows, :] + tile
        ref[rows * z : rows * z + rows, :] = tile


def put_gram(ref, core, gram_ref):
    half = gram_ref[core]
    ref[ref.shape[0] - half.shape[0] :, :] = half


def begin_kernel(parts, share, s_hbm, e_hbm, theirs_ref, sketched_ref, gram_ref, e_ref, *scratch):
    s_ref, acc, sems = scratch
    count = len(PIECES)
    spans = [slice(sum(PIECES[:i]), sum(PIECES[: i + 1])) for i in range(count)]
    blocks = [slice(sum(BLOCKS[:j]), sum(BLOCKS[: j + 1])) for j in range(len(BLOCKS))]
    whole = pltpu.make_async_copy(s_hbm, s_ref, sems.at[count * len(BLOCKS)])
    whole.start()
    copies = []
    for j, block in enumerate(blocks):
        for i, span in enumerate(spans):
            where = (pl.ds(span.start, PIECES[i]), pl.ds(block.start, BLOCKS[j]))
            copy = pltpu.make_async_copy(e_hbm.at[where], e_ref.at[where], sems.at[j * count + i])
            copy.start()
            copies.append(copy)
    whole.wait()
    core, _, half = place()
    core, half = 1 - core, 1 - half
    square = None
    for j, block in enumerate(blocks):
        for i, span in enumerate(spans):
            copies[j * count + i].wait()
            term = nn(s_ref[:, span], e_ref[span, block])
            if i > 0:
                term = acc[:, : BLOCKS[j]] + term
            if i < count - 1:
                acc[:, : BLOCKS[j]] = term
        sketched = term.astype(jnp.bfloat16)
        sketched_ref[:, block] = sketched
        term = nt(sketched, sketched)
        square = term if j == 0 else square + term
        put_products(theirs_ref, core, half, parts, share, sketched, e_ref, block, j > 0)
    quarter = square.shape[0] // 4
    for h in range(2):
        top = square[2 * quarter * h : 2 * quarter * h + quarter]
        low = square[2 * quarter * h + quarter : 2 * quarter * (h + 1)]
        gram_ref[h] = jnp.concatenate([top, low], axis=1)
    put_gram(theirs_ref, core, gram_ref)


def more_kernel(which, parts, share, sketched_ref, gram_ref, e_ref, out_ref):
    core, kept, across = place()
    core, half = {"give": (core, 1 - kept), "keep": (core, kept), "theirs": (1 - core, across)}[which]
    put_gram(out_ref, core, gram_ref)
    put_products(out_ref, core, half, parts, share, sketched_ref[...], e_ref)


def begin(sketch_map, expression, parts):
    rows, genes = sketch_map.shape
    cells = expression.shape[1]
    return pl.pallas_call(
        functools.partial(begin_kernel, parts, genes // parts),
        in_specs=[pl.BlockSpec(memory_space=pltpu.HBM)] * 2,
        out_specs=[pl.BlockSpec(memory_space=pltpu.VMEM)] * 4,
        out_shape=[
            pltpu.VMEM((rows * parts + rows // 4, 128), jnp.float32),
            pltpu.VMEM((rows, cells), jnp.bfloat16),
            pltpu.VMEM((2, rows // 4, 128), jnp.float32),
            pltpu.VMEM((genes, cells), jnp.bfloat16),
        ],
        scratch_shapes=[
            pltpu.VMEM((rows, genes), jnp.bfloat16),
            pltpu.VMEM((rows, max(BLOCKS)), jnp.float32),
            pltpu.SemaphoreType.DMA((len(PIECES) * len(BLOCKS) + 1,)),
        ],
        compiler_params=pltpu.CompilerParams(vmem_limit_bytes=16 << 20),
        name="begin",
    )(
        pltpu.with_memory_space_constraint(sketch_map, pltpu.HBM),
        pltpu.with_memory_space_constraint(expression, pltpu.HBM),
    )


def more(which, sketched, gram, expression, parts):
    genes, cells = expression.shape
    rows = sketched.shape[0]
    return pl.pallas_call(
        functools.partial(more_kernel, which, parts, genes // parts),
        in_specs=[pl.BlockSpec(memory_space=pltpu.VMEM)] * 3,
        out_specs=pl.BlockSpec(memory_space=pltpu.VMEM),
        out_shape=pltpu.VMEM((rows * parts + rows // 4, 128), jnp.float32),
        cost_estimate=pl.CostEstimate(
            flops=rows * genes * cells // 2, bytes_accessed=genes * cells, transcendentals=0
        ),
        compiler_params=pltpu.CompilerParams(vmem_limit_bytes=8 << 20),
        name=which,
    )(near(sketched), near(gram), near(expression))


def small(kernel, shape, name, *args, space=jax.ShapeDtypeStruct):
    return pl.pallas_call(
        kernel,
        in_specs=[pl.BlockSpec(memory_space=pltpu.VMEM)] * len(args),
        out_specs=pl.BlockSpec(memory_space=pltpu.VMEM),
        out_shape=space(shape, jnp.float32),
        name=name,
    )(*args)


def over_tile(x):
    return jnp.broadcast_to(x, (8, 128))


def inverse_factor(work, sub):
    count = len(work)
    for g in range(count):
        block = work[g]
        at = 64 + 8 * g
        columns = [over_tile(block[:, at + j : at + j + 1]) for j in range(8)]
        a = {(i, j): over_tile(columns[j][i : i + 1]) for j in range(8) for i in range(j, 8)}
        rows = [over_tile(block[i : i + 1]) for i in range(8)]
        low, inverse = {}, []
        for j in range(8):
            inverse.append(1.0 / a[j, j])
            for i in range(j + 1, 8):
                low[i, j] = a[i, j] * inverse[j]
            for i in range(j + 1, 8):
                for m in range(j + 1, i + 1):
                    a[i, m] = a[i, m] - low[i, j] * a[m, j]
        solved = []
        for i in range(8):
            row = rows[i]
            for j in range(i):
                row = row - low[i, j] * solved[j]
            solved.append(row)
        if g < count - 1:
            back = [None] * 8
            for i in reversed(range(8)):
                row = solved[i] * inverse[i]
                for j in range(i + 1, 8):
                    row = row - low[j, i] * back[j]
                back[i] = row
            for h in range(g + 1, count):
                left = work[h]
                for j in range(8):
                    left = left - over_tile(work[h][:, at + j : at + j + 1]) * back[j]
                work[h] = left
        block, pivots = solved[0], a[0, 0]
        for i in range(1, 8):
            block = jnp.where(sub == i, solved[i], block)
            pivots = jnp.where(sub == i, a[i, i], pivots)
        work[g] = block * lax.rsqrt(pivots)
    return work


def factor_kernel(mine_ref, other_ref, out_ref):
    me = place()[0]
    mine, other = mine_ref[...], other_ref[...]
    halves = [jnp.where(me == 0, mine, other), jnp.where(me == 0, other, mine)]
    sub = lax.broadcasted_iota(jnp.int32, (8, 128), 0)
    lane = lax.broadcasted_iota(jnp.int32, (8, 128), 1)
    work = []
    for g in range(8):
        held = halves[g // 4][8 * (g % 2) : 8 * (g % 2) + 8]
        if g // 2 % 2 == 0:
            held = pltpu.roll(held, 64, 1)
        work.append(jnp.where(lane < 64, jnp.where(lane == sub + 8 * g, 1.0, 0.0), held))
    for g, block in enumerate(inverse_factor(work, sub)):
        out_ref[8 * g : 8 * g + 8, :] = block[:, :64]


def solve(inverse_ref, columns):
    return lax.dot_general(
        inverse_ref[...],
        columns,
        (((1,), (0,)), ((), ())),
        precision=lax.Precision.HIGHEST,
        preferred_element_type=jnp.float32,
    )


def own_kernel(inverse_ref, mine_ref, out_ref):
    rows = out_ref.shape[0]
    out_ref[...] = solve(
        inverse_ref, jnp.concatenate([mine_ref[:rows], mine_ref[rows:]], axis=1)
    )


def apply_kernel(parts, inverse_ref, own_ref, other_ref, out_ref):
    rows, share = out_ref.shape
    core, kept, across = place()
    other = solve(inverse_ref, jnp.concatenate([other_ref[:rows], other_ref[rows:]], axis=1))
    mine = [own_ref[:, :128], own_ref[:, 128:]]
    other = [other[:, :128], other[:, 128:]]
    mine = [jnp.where(kept == t, mine[0], mine[1]) for t in range(2)]
    other = [jnp.where(across == t, other[0], other[1]) for t in range(2)]
    tiles = [jnp.where(core == 0, p, q) for p, q in zip(mine + other, other + mine)]
    solved = jnp.concatenate(tiles, axis=1)
    extra = lax.axis_index("narrow") * share % 16
    for shift in sorted({z * share % 16 for z in range(parts)}):

        @pl.when(extra == shift)
        def _():
            out_ref[...] = solved[:, shift : shift + share]


def near(x):
    return pltpu.with_memory_space_constraint(x, pltpu.VMEM)


def wide_index(y, x, core):
    return (y * 4 + x) * 2 + core


def neighbours():
    return [
        (wide_index(y, x, core), wide_index(y ^ core, x ^ 1 ^ core, core))
        for y in range(4)
        for x in range(4)
        for core in range(2)
    ]


def holders():
    return [
        [wide_index(*((v, u) if core == 0 else (u, v)), core) for v in range(4) for u in (a, 3 - a)]
        for core in range(2)
        for a in range(2)
    ]


def on_device(expression, sketch_map):
    rows, genes = sketch_map.shape
    parts = lax.axis_size("narrow")
    swap = [(i, i ^ 1) for i in range(lax.axis_size("wide"))]
    pairs, groups = neighbours(), holders()
    theirs, sketched, gram, held = begin(sketch_map, expression, parts)
    theirs = lax.ppermute(theirs, "wide", swap)
    give = more("give", sketched, gram, held, parts) + theirs
    give, gram = lax.optimization_barrier((give, gram))
    given = lax.ppermute(give, "wide", pairs)
    theirs = lax.ppermute(more("theirs", sketched, gram, held, parts), "wide", swap)
    keep = lax.optimization_barrier(more("keep", sketched, gram, held, parts) + given)
    half = keep + theirs
    ours = half[: rows * parts].reshape(parts, rows, 128)
    square = jnp.broadcast_to(half[None, rows * parts :], (parts, rows // 4, 128))
    piece = jnp.concatenate([ours, square], axis=1)
    piece = lax.all_to_all(piece, "narrow", 0, 0, tiled=True).sum(axis=0)
    spread = jnp.broadcast_to(piece[None], (len(groups[0]), *piece.shape))
    spread = lax.all_to_all(spread, "wide", 0, 0, axis_index_groups=groups, tiled=True)
    total = spread.sum(axis=0)
    ours, square = total[:rows], total[rows:]
    beside = lax.ppermute(ours, "wide", pairs)
    inverse = small(
        factor_kernel,
        (rows, rows),
        "factor",
        near(square),
        near(lax.ppermute(square, "wide", swap)),
        space=pltpu.VMEM,
    )
    beside, inverse = lax.optimization_barrier((beside, inverse))
    mine = jnp.concatenate([ours, beside], axis=0)
    other = near(lax.ppermute(mine, "wide", swap))
    own = small(own_kernel, (rows, SPAN), "own", near(inverse), near(mine), space=pltpu.VMEM)
    return small(
        functools.partial(apply_kernel, parts),
        (rows, genes // parts),
        "apply",
        near(inverse),
        near(own),
        other,
    )


def solution(mesh):
    placed = (P(None, ("wide", "narrow")), P())
    return jax.shard_map(
        on_device, mesh=mesh, in_specs=placed, out_specs=P(None, "narrow"), check_vma=False
    )
```

```python
import functools

import jax
import jax.numpy as jnp
from jax import lax
from jax.experimental import pallas as pl
from jax.experimental.pallas import tpu as pltpu
from jax.sharding import PartitionSpec as P

PIECES = (1024, 1024, 1024, 928)
BLOCKS = (512, 512, 512)
SPAN = 256


def nn(a, b):
    return lax.dot_general(a, b, (((1,), (0,)), ((), ())), preferred_element_type=jnp.float32)


def nt(a, b):
    return lax.dot_general(a, b, (((1,), (1,)), ((), ())), preferred_element_type=jnp.float32)


def window_start(z, share):
    return z * share // 16 * 16


def place():
    index = lax.axis_index("wide")
    core, x, y = index & 1, (index >> 1) & 3, index >> 3
    along_x, along_y = (x ^ (x >> 1)) & 1, (y ^ (y >> 1)) & 1
    return core, jnp.where(core == 0, along_x, along_y), jnp.where(core == 0, along_y, along_x)


def put_products(ref, core, half, parts, share, sketched, e_ref, cells=slice(None), add=False):
    rows = sketched.shape[0]
    for z in range(parts):
        start = pl.multiple_of(window_start(z, share) + SPAN * core + SPAN // 2 * half, 16)
        tile = nt(sketched, e_ref[pl.ds(start, SPAN // 2), cells])
        if add:
            tile = ref[rows * z : rows * z + rows, :] + tile
        ref[rows * z : rows * z + rows, :] = tile


def put_gram(ref, core, gram_ref):
    half = gram_ref[core]
    ref[ref.shape[0] - half.shape[0] :, :] = half


def begin_kernel(parts, share, s_hbm, e_hbm, theirs_ref, sketched_ref, gram_ref, e_ref, *scratch):
    s_ref, acc, sems = scratch
    count = len(PIECES)
    spans = [slice(sum(PIECES[:i]), sum(PIECES[: i + 1])) for i in range(count)]
    blocks = [slice(sum(BLOCKS[:j]), sum(BLOCKS[: j + 1])) for j in range(len(BLOCKS))]
    whole = pltpu.make_async_copy(s_hbm, s_ref, sems.at[count * len(BLOCKS)])
    whole.start()
    copies = []
    for j, block in enumerate(blocks):
        for i, span in enumerate(spans):
            where = (pl.ds(span.start, PIECES[i]), pl.ds(block.start, BLOCKS[j]))
            copy = pltpu.make_async_copy(e_hbm.at[where], e_ref.at[where], sems.at[j * count + i])
            copy.start()
            copies.append(copy)
    whole.wait()
    core, _, half = place()
    core, half = 1 - core, 1 - half
    square = None
    for j, block in enumerate(blocks):
        for i, span in enumerate(spans):
            copies[j * count + i].wait()
            term = nn(s_ref[:, span], e_ref[span, block])
            if i > 0:
                term = acc[:, : BLOCKS[j]] + term
            if i < count - 1:
                acc[:, : BLOCKS[j]] = term
        sketched = term.astype(jnp.bfloat16)
        sketched_ref[:, block] = sketched
        term = nt(sketched, sketched)
        square = term if j == 0 else square + term
        put_products(theirs_ref, core, half, parts, share, sketched, e_ref, block, j > 0)
    quarter = square.shape[0] // 4
    for h in range(2):
        top = square[2 * quarter * h : 2 * quarter * h + quarter]
        low = square[2 * quarter * h + quarter : 2 * quarter * (h + 1)]
        gram_ref[h] = jnp.concatenate([top, low], axis=1)
    put_gram(theirs_ref, core, gram_ref)


def more_kernel(which, parts, share, sketched_ref, gram_ref, e_ref, out_ref):
    core, kept, across = place()
    core, half = {"give": (core, 1 - kept), "keep": (core, kept), "theirs": (1 - core, across)}[which]
    put_gram(out_ref, core, gram_ref)
    put_products(out_ref, core, half, parts, share, sketched_ref[...], e_ref)


def begin(sketch_map, expression, parts):
    rows, genes = sketch_map.shape
    cells = expression.shape[1]
    return pl.pallas_call(
        functools.partial(begin_kernel, parts, genes // parts),
        in_specs=[pl.BlockSpec(memory_space=pltpu.HBM)] * 2,
        out_specs=[pl.BlockSpec(memory_space=pltpu.VMEM)] * 4,
        out_shape=[
            pltpu.VMEM((rows * parts + rows // 4, 128), jnp.float32),
            pltpu.VMEM((rows, cells), jnp.bfloat16),
            pltpu.VMEM((2, rows // 4, 128), jnp.float32),
            pltpu.VMEM((genes, cells), jnp.bfloat16),
        ],
        scratch_shapes=[
            pltpu.VMEM((rows, genes), jnp.bfloat16),
            pltpu.VMEM((rows, max(BLOCKS)), jnp.float32),
            pltpu.SemaphoreType.DMA((len(PIECES) * len(BLOCKS) + 1,)),
        ],
        compiler_params=pltpu.CompilerParams(vmem_limit_bytes=16 << 20),
        name="begin",
    )(
        pltpu.with_memory_space_constraint(sketch_map, pltpu.HBM),
        pltpu.with_memory_space_constraint(expression, pltpu.HBM),
    )


def more(which, sketched, gram, expression, parts):
    genes, cells = expression.shape
    rows = sketched.shape[0]
    return pl.pallas_call(
        functools.partial(more_kernel, which, parts, genes // parts),
        in_specs=[pl.BlockSpec(memory_space=pltpu.VMEM)] * 3,
        out_specs=pl.BlockSpec(memory_space=pltpu.VMEM),
        out_shape=pltpu.VMEM((rows * parts + rows // 4, 128), jnp.float32),
        cost_estimate=pl.CostEstimate(
            flops=rows * genes * cells // 2, bytes_accessed=genes * cells, transcendentals=0
        ),
        compiler_params=pltpu.CompilerParams(vmem_limit_bytes=8 << 20),
        name=which,
    )(near(sketched), near(gram), near(expression))


def small(kernel, shape, name, *args, space=jax.ShapeDtypeStruct):
    return pl.pallas_call(
        kernel,
        in_specs=[pl.BlockSpec(memory_space=pltpu.VMEM)] * len(args),
        out_specs=pl.BlockSpec(memory_space=pltpu.VMEM),
        out_shape=space(shape, jnp.float32),
        name=name,
    )(*args)


def over_tile(x):
    return jnp.broadcast_to(x, (8, 128))


def inverse_factor(work, sub):
    count = len(work)
    for g in range(count):
        block = work[g]
        at = 64 + 8 * g
        columns = [over_tile(block[:, at + j : at + j + 1]) for j in range(8)]
        a = {(i, j): over_tile(columns[j][i : i + 1]) for j in range(8) for i in range(j, 8)}
        rows = [over_tile(block[i : i + 1]) for i in range(8)]
        low, inverse = {}, []
        for j in range(8):
            inverse.append(1.0 / a[j, j])
            for i in range(j + 1, 8):
                low[i, j] = a[i, j] * inverse[j]
            for i in range(j + 1, 8):
                for m in range(j + 1, i + 1):
                    a[i, m] = a[i, m] - low[i, j] * a[m, j]
        solved = []
        for i in range(8):
            row = rows[i]
            for j in range(i):
                row = row - low[i, j] * solved[j]
            solved.append(row)
        if g < count - 1:
            back = [None] * 8
            for i in reversed(range(8)):
                row = solved[i] * inverse[i]
                for j in range(i + 1, 8):
                    row = row - low[j, i] * back[j]
                back[i] = row
            for h in range(g + 1, count):
                left = work[h]
                for j in range(8):
                    left = left - over_tile(work[h][:, at + j : at + j + 1]) * back[j]
                work[h] = left
        block, pivots = solved[0], a[0, 0]
        for i in range(1, 8):
            block = jnp.where(sub == i, solved[i], block)
            pivots = jnp.where(sub == i, a[i, i], pivots)
        work[g] = block * lax.rsqrt(pivots)
    return work


def factor_kernel(mine_ref, other_ref, out_ref):
    me = place()[0]
    mine, other = mine_ref[...], other_ref[...]
    halves = [jnp.where(me == 0, mine, other), jnp.where(me == 0, other, mine)]
    sub = lax.broadcasted_iota(jnp.int32, (8, 128), 0)
    lane = lax.broadcasted_iota(jnp.int32, (8, 128), 1)
    work = []
    for g in range(8):
        held = halves[g // 4][8 * (g % 2) : 8 * (g % 2) + 8]
        if g // 2 % 2 == 0:
            held = pltpu.roll(held, 64, 1)
        work.append(jnp.where(lane < 64, jnp.where(lane == sub + 8 * g, 1.0, 0.0), held))
    for g, block in enumerate(inverse_factor(work, sub)):
        out_ref[8 * g : 8 * g + 8, :] = block[:, :64]


def apply_kernel(parts, inverse_ref, mine_ref, other_ref, out_ref):
    rows, share = out_ref.shape
    core, kept, across = place()
    mine = [mine_ref[:rows], mine_ref[rows:]]
    other = [other_ref[:rows], other_ref[rows:]]
    mine = [jnp.where(kept == t, mine[0], mine[1]) for t in range(2)]
    other = [jnp.where(across == t, other[0], other[1]) for t in range(2)]
    tiles = [jnp.where(core == 0, p, q) for p, q in zip(mine + other, other + mine)]
    solved = lax.dot_general(
        inverse_ref[...],
        jnp.concatenate(tiles, axis=1),
        (((1,), (0,)), ((), ())),
        precision=lax.Precision.HIGHEST,
        preferred_element_type=jnp.float32,
    )
    extra = lax.axis_index("narrow") * share % 16
    for shift in sorted({z * share % 16 for z in range(parts)}):

        @pl.when(extra == shift)
        def _():
            out_ref[...] = solved[:, shift : shift + share]


def near(x):
    return pltpu.with_memory_space_constraint(x, pltpu.VMEM)


def wide_index(y, x, core):
    return (y * 4 + x) * 2 + core


def neighbours():
    return [
        (wide_index(y, x, core), wide_index(y ^ core, x ^ 1 ^ core, core))
        for y in range(4)
        for x in range(4)
        for core in range(2)
    ]


def holders():
    return [
        [wide_index(*((v, u) if core == 0 else (u, v)), core) for v in range(4) for u in (a, 3 - a)]
        for core in range(2)
        for a in range(2)
    ]


def on_device(expression, sketch_map):
    rows, genes = sketch_map.shape
    parts = lax.axis_size("narrow")
    swap = [(i, i ^ 1) for i in range(lax.axis_size("wide"))]
    pairs, groups = neighbours(), holders()
    theirs, sketched, gram, held = begin(sketch_map, expression, parts)
    theirs = lax.ppermute(theirs, "wide", swap)
    give = more("give", sketched, gram, held, parts) + theirs
    give, gram = lax.optimization_barrier((give, gram))
    given = lax.ppermute(give, "wide", pairs)
    theirs = lax.ppermute(more("theirs", sketched, gram, held, parts), "wide", swap)
    keep = lax.optimization_barrier(more("keep", sketched, gram, held, parts) + given)
    half = keep + theirs
    ours = half[: rows * parts].reshape(parts, rows, 128)
    square = jnp.broadcast_to(half[None, rows * parts :], (parts, rows // 4, 128))
    piece = jnp.concatenate([ours, square], axis=1)
    piece = lax.all_to_all(piece, "narrow", 0, 0, tiled=True).sum(axis=0)
    spread = jnp.broadcast_to(piece[None], (len(groups[0]), *piece.shape))
    spread = lax.all_to_all(spread, "wide", 0, 0, axis_index_groups=groups, tiled=True)
    total = spread.sum(axis=0)
    ours, square = total[:rows], total[rows:]
    beside = lax.ppermute(ours, "wide", pairs)
    theirs = lax.ppermute(total, "wide", swap)
    inverse = small(
        factor_kernel, (rows, rows), "factor", near(square), near(theirs[rows:]), space=pltpu.VMEM
    )
    beside, inverse = lax.optimization_barrier((beside, inverse))
    mine = jnp.concatenate([ours, beside], axis=0)
    other = jnp.concatenate([theirs[:rows], lax.ppermute(beside, "wide", swap)], axis=0)
    return small(
        functools.partial(apply_kernel, parts),
        (rows, genes // parts),
        "apply",
        near(inverse),
        near(mine),
        near(other),
    )


def solution(mesh):
    placed = (P(None, ("wide", "narrow")), P())
    return jax.shard_map(
        on_device, mesh=mesh, in_specs=placed, out_specs=P(None, "narrow"), check_vma=False
    )
```
